512 devices in a mesh: comp: 4 (over y_hi, core), tile: 128 (over z, y_lo, x).
Axes of the slice: x: 4, y: 4 (y_hi: 2, y_lo: 2; y = y_hi * 2 + y_lo), z: 16, core: 2. Of those that a mesh axis runs over, the one named last changes fastest.
Arguments:
- column_state: float32 [4, 128, 4, 16, 2048], P('comp', 'tile'), may hold values from -6 to 6
- mixing: float32 [2, 4, 16], replicated, may hold values from 0.02 to 0.24
- vertical: float32 [2, 16, 16], replicated, may hold values from -1.5 to 1.5
- flux_coef: float32 [2, 4], replicated, may hold values from 0.5 to 1.5
- atm_block: int32 [4, 128, 16], P('comp', 'tile'), may hold values from 0 to 15
- ocean_block: int32 [4, 128, 16], P('comp', 'tile'), may hold values from 0 to 15
- tile_offset: int32 [4, 128, 16], P('comp', 'tile'), may hold values from 0 to 6
- remap_weights: bfloat16 [4, 128, 16, 128, 128], P('comp', 'tile'), may hold values from 0 to 0.119628906
- ocean_mask: int32 [128, 2048], P('tile'), may hold values 0 or 1
Outputs:
- new_state: float32 [4, 128, 4, 16, 2048], P('comp', 'tile')
The draws below stay inside these ranges and needn't reach their ends.
Inputs may be any that keep to these rules, and one draw needn't show every extreme that they name: `atm_block`: entries at comp index 3 are not read.
All inputs are finite; a program needn't handle non-finite values. No bound on the sum of `ocean_mask` on one device may be relied on, other than what follows from the above.
Results may differ from the reference program's by a relative error of at most 0.0003.
Values sent between devices are 32-bit elements; how exact they have to be, the bound alone decides.
A program may use at most 64 MiB of HBM per device.

```python
import math
import jax
import jax.numpy as jnp
from jax import lax

LEV = 16
K = 4
BA = 128
BO = 128
AB = 16
REACH = 3
SUB = 2
CELLS = 2048
OB = 16
NB = 16
N_COMP = 4
N_TILE = 128


def with_ends(entries, own_key, least, high):
    spot = [jax.random.randint(jax.random.fold_in(own_key, axis), (), 0, length) for axis, length in enumerate(entries.shape)]
    longest = entries.shape.index(max(entries.shape))
    beside = spot[:longest] + [(spot[longest] + 1) % entries.shape[longest]] + spot[longest + 1:]
    return entries.at[tuple(spot)].set(least).at[tuple(beside)].set(high)


def levels(stream_key, shape, pieces, smallest, high):
    def one(position, shards_of):
        heights = jax.random.uniform(jax.random.fold_in(jax.random.fold_in(stream_key, 6), position), (shards_of,), jnp.float32, smallest / len(pieces), high / len(pieces))
        return jnp.repeat(jnp.exp(heights), shape[position] // shards_of).reshape((-1,) + (1,) * (len(shape) - position - 1))

    level = one(*pieces[0])
    for cut in pieces[1:]:
        level = level * one(*cut)
    return level


def noise(own_key, shape, deviation, bound, shards=(), kind=jnp.bfloat16):
    values = jax.random.normal(own_key, shape, jnp.float32) * deviation
    if len(shards) > 0:
        values = levels(own_key, shape, shards, -0.22, 0.18) * values
    return jnp.clip(values, min=-bound, max=bound).astype(kind)


def setup_inputs(seed: int = 0) -> dict:
    key_list = jax.random.split(jax.random.key(seed), 10)
    return {
        "column_state": noise(key_list[0], (N_COMP, N_TILE, K, LEV, CELLS), 1.0, 6.0, ((0, 4), (1, 128)), jnp.float32),
        "mixing": jnp.clip(jnp.exp(jax.random.uniform(key_list[1], (2, K, LEV), jnp.float32, math.log(0.02), math.log(0.24))), 0.02, 0.24),
        "vertical": noise(key_list[2], (2, LEV, LEV), LEV ** -0.5, 1.5, (), jnp.float32),
        "flux_coef": jnp.clip(jax.random.uniform(key_list[3], (2, K), jnp.float32, 0.5, 1.5), 0.5, 1.5),
        "atm_block": with_ends(jax.random.randint(key_list[4], (N_COMP, N_TILE, NB), 0, AB), jax.random.fold_in(key_list[4], 1), 0, AB - 1).astype(jnp.int32),
        "ocean_block": with_ends(jax.random.randint(key_list[5], (N_COMP, N_TILE, NB), 0, OB), jax.random.fold_in(key_list[5], 1), 0, OB - 1).astype(jnp.int32),
        "tile_offset": with_ends(jax.random.randint(key_list[6], (N_COMP, N_TILE, NB), 0, 2 * REACH + 1), jax.random.fold_in(key_list[6], 1), 0, 2 * REACH).astype(jnp.int32),
        "remap_weights": jnp.clip(0.119628906 * jax.random.uniform(key_list[7], (N_COMP, N_TILE, NB, BA, BO), jnp.float32) ** levels(key_list[7], (N_COMP, N_TILE, NB, BA, BO), ((0, 4), (1, 128)), -0.2, 0.2), 0.0, 0.119628906).astype(jnp.bfloat16),
        "ocean_mask": with_ends((jax.random.randint(key_list[8], (N_TILE, CELLS), 0, 4) < 3).astype(jnp.int32), jax.random.fold_in(key_list[8], 1), 0, 1),
    }


def remap_row(row):
    blocks, chosen_index, target_block, offsets, weights = row
    tiles = blocks.shape[1]
    picked = blocks[:, jnp.arange(tiles, dtype=jnp.int32)[:, None], chosen_index]
    contrib = jnp.einsum('ktnb,tnbj->tnkj', picked.astype(jnp.float32), weights.astype(jnp.float32), precision=lax.Precision.HIGHEST)
    destination = (jnp.arange(tiles, dtype=jnp.int32)[:, None] + offsets - REACH) % tiles
    empty = jnp.zeros((tiles, OB, K, BO), jnp.float32)
    return empty.at[destination, target_block].add(contrib)


def reference(column_state, mixing, vertical, flux_coef, atm_block, ocean_block, tile_offset, remap_weights, ocean_mask):
    comps = column_state.shape[0]
    tiles = column_state.shape[1]
    atmos_rows = comps - 1
    fields = jnp.moveaxis(column_state, 1, 3).reshape(comps, K, LEV, tiles * CELLS)
    is_atmos = (jnp.arange(comps, dtype=jnp.int32) < atmos_rows)
    rates = jnp.where(is_atmos[:, None, None, None], mixing[0][None, :, :, None], mixing[1][None, :, :, None])
    for sweep in range(SUB):
        laplace = jnp.roll(fields, 1, axis=3) + jnp.roll(fields, -1, axis=3) - 2.0 * fields
        fields = fields + rates * laplace
    operators = jnp.where(is_atmos[:, None, None], vertical[0][None], vertical[1][None])
    mixed = fields + jnp.einsum('clm,ckmz->cklz', operators, fields, precision=lax.Precision.HIGHEST)
    atmos_mixed = mixed[:atmos_rows]
    ocean_cycle = mixed[atmos_rows]
    surface = jnp.tanh(flux_coef[0][None, :, None] * atmos_mixed[:, :, LEV - 1] + flux_coef[1][None, :, None] * atmos_mixed[:, :, LEV - 2])
    rounded = surface.astype(jnp.bfloat16)
    blocks = rounded.reshape(atmos_rows, K, tiles, AB, BA)
    totals = lax.map(remap_row, (blocks, atm_block[:atmos_rows], ocean_block[:atmos_rows], tile_offset[:atmos_rows], remap_weights[:atmos_rows])).sum(0)
    received = totals.transpose(2, 0, 1, 3).reshape(K, tiles * CELLS)
    land = ocean_mask.reshape(tiles * CELLS).astype(jnp.float32)
    atmosphere = atmos_mixed.at[:, :, LEV - 1].add(-0.5 * surface)
    ocean = ocean_cycle.at[:, 0].add(land[None, :] * received)
    whole = jnp.concatenate([atmosphere, ocean[None]], axis=0)
    return jnp.moveaxis(whole.reshape(comps, K, LEV, tiles, CELLS), 3, 1)
```

```python
import functools

import jax
import jax.numpy as jnp
from jax import lax
from jax.experimental import pallas as pl
from jax.experimental.pallas import tpu as pltpu
from jax.sharding import PartitionSpec as P

REACH = 3
SPREAD = 2 * REACH + 1
MESH = pl.DeviceIdType.MESH
F32 = jnp.float32
BF16 = jnp.bfloat16
LANES = 128
SURF = 16


def iota(shape, dim):
    return lax.broadcasted_iota(jnp.int32, shape, dim)


def column(row, count):
    wide = jnp.broadcast_to(row, (count, row.shape[1]))
    keep = iota(wide.shape, 0) == iota(wide.shape, 1)
    return jnp.sum(jnp.where(keep, wide, 0.0), axis=1, keepdims=True)


def split2(x):
    hi = x.astype(BF16)
    lo = (x - hi.astype(F32)).astype(BF16)
    return hi, lo


def kernel(
    dims,
    state,
    mixing,
    vertical,
    flux,
    ablk,
    oblk,
    toff,
    weights,
    mask,
    out,
    f,
    mix_v,
    ver_v,
    flux_v,
    ablk_s,
    oblk_v,
    toff_v,
    w_v,
    mask_v,
    coef,
    opmat,
    pack,
    halo,
    surf,
    contrib,
    dense,
    recv,
    rx,
    load_sem,
    halo_send,
    halo_recv,
    dense_send,
    dense_recv,
):
    fields, lev, cells, comps, tiles, nb = dims
    rows = fields * lev
    ntile = cells // LANES
    oblocks = cells // LANES
    c = lax.axis_index("comp")
    t = lax.axis_index("tile")
    ocean_row = comps - 1
    is_atmos = c < ocean_row
    is_ocean = c == ocean_row
    group = jnp.where(is_atmos, 0, 1)
    left = lax.rem(t + tiles - 1, tiles)
    right = lax.rem(t + 1, tiles)

    loads = [
        pltpu.make_async_copy(state.at[:, pl.ds(0, LANES)], f.at[:, pl.ds(LANES, LANES)], load_sem.at[0]),
        pltpu.make_async_copy(
            state.at[:, pl.ds(cells - LANES, LANES)], f.at[:, pl.ds(cells, LANES)], load_sem.at[1]
        ),
        pltpu.make_async_copy(
            state.at[:, pl.ds(LANES, cells - 2 * LANES)],
            f.at[:, pl.ds(2 * LANES, cells - 2 * LANES)],
            load_sem.at[2],
        ),
        pltpu.make_async_copy(mixing, mix_v, load_sem.at[3]),
        pltpu.make_async_copy(vertical, ver_v, load_sem.at[4]),
        pltpu.make_async_copy(flux, flux_v, load_sem.at[5]),
        pltpu.make_async_copy(ablk, ablk_s, load_sem.at[6]),
        pltpu.make_async_copy(oblk, oblk_v, load_sem.at[7]),
        pltpu.make_async_copy(toff, toff_v, load_sem.at[8]),
        pltpu.make_async_copy(weights, w_v, load_sem.at[9]),
        pltpu.make_async_copy(mask, mask_v, load_sem.at[10]),
    ]
    barrier = pltpu.get_barrier_semaphore()
    for who in (left, right):
        pl.semaphore_signal(barrier, inc=1, device_id=(c, who), device_id_type=MESH)
    for load in loads:
        load.start()

    @pl.when(is_ocean)
    def _():
        for src in range(comps - 1):
            for d in range(-REACH, REACH + 1):
                who = lax.rem(t - d + tiles, tiles)
                pl.semaphore_signal(barrier, inc=1, device_id=(src, who), device_id_type=MESH)

    loads[0].wait()
    loads[1].wait()
    lane = iota((8, LANES), 1)
    groups = rows // 8
    first = jnp.zeros((8, LANES), F32)
    last = jnp.zeros((8, LANES), F32)
    for i in range(groups):
        here = lane // 2 == i
        a = f[8 * i : 8 * i + 8, LANES : 2 * LANES]
        b = f[8 * i : 8 * i + 8, cells : cells + LANES]
        first = jnp.where(here, pltpu.roll(a, 2 * i, 1) if i else a, first)
        last = jnp.where(here, pltpu.roll(b, 2 * i + 2, 1), last)
    pack[0] = first
    pack[1] = last

    loads[3].wait()
    loads[4].wait()
    loads[5].wait()
    mix_g = mix_v[group]
    rates = jnp.concatenate([column(mix_g[k : k + 1, :], lev) for k in range(fields)], axis=0)
    keep = 1.0 - 2.0 * rates
    coef[0] = jnp.broadcast_to(keep * keep + 2.0 * rates * rates, (rows, LANES))
    coef[1] = jnp.broadcast_to(2.0 * rates * keep, (rows, LANES))
    coef[2] = jnp.broadcast_to(rates * rates, (rows, LANES))
    ver_g = ver_v[group]
    spread_l = (lax.rem(iota((rows, lev), 0), lev) == iota((rows, lev), 1)).astype(F32)
    spread_r = (lax.rem(iota((lev, rows), 1), lev) == iota((lev, rows), 0)).astype(F32)
    hp = lax.Precision.HIGHEST
    tall = jnp.dot(spread_l, ver_g, precision=hp, preferred_element_type=F32)
    square = jnp.dot(tall, spread_r, precision=hp, preferred_element_type=F32)
    square = jnp.where(iota((rows, rows), 0) // lev == iota((rows, rows), 1) // lev, square, 0.0)
    fa = jnp.concatenate([column(flux_v[0:1, :], fields), jnp.zeros((SURF - fields, 1), F32)], axis=0)
    fb = jnp.concatenate([column(flux_v[1:2, :], fields), jnp.zeros((SURF - fields, 1), F32)], axis=0)
    who_row, who_col = iota((SURF, rows), 0), iota((SURF, rows), 1)
    pick = jnp.where(who_col == who_row * lev + lev - 1, fa, 0.0) + jnp.where(
        who_col == who_row * lev + lev - 2, fb, 0.0
    )
    linear = pick + jnp.dot(pick, square, precision=hp, preferred_element_type=F32)
    high = rows + SURF
    sq_hi, sq_lo = split2(jnp.concatenate([square, linear], axis=0))
    opmat[0:high] = sq_hi
    opmat[high : 2 * high] = sq_lo
    half = jnp.where(is_atmos, 0.5, 0.0)

    pl.semaphore_wait(barrier, jnp.where(is_atmos, 2 + SPREAD, 2))
    to_right = pltpu.make_async_remote_copy(
        src_ref=pack.at[1],
        dst_ref=halo.at[0],
        send_sem=halo_send.at[0],
        recv_sem=halo_recv.at[0],
        device_id=(c, right),
        device_id_type=MESH,
    )
    to_left = pltpu.make_async_remote_copy(
        src_ref=pack.at[0],
        dst_ref=halo.at[1],
        send_sem=halo_send.at[1],
        recv_sem=halo_recv.at[1],
        device_id=(c, left),
        device_id_type=MESH,
    )
    to_right.start()
    to_left.start()

    def stencil(x, i):
        n = x.shape[1]
        s = slice(8 * i, 8 * i + 8)
        wide = lambda v: jnp.concatenate([v] * (n // LANES), axis=1)
        near = pltpu.roll(x, 1, 1) + pltpu.roll(x, n - 1, 1)
        far = pltpu.roll(x, 2, 1) + pltpu.roll(x, n - 2, 1)
        return wide(coef[0, s]) * x + wide(coef[1, s]) * near + wide(coef[2, s]) * far

    def mix(x, spots):
        hi, lo = split2(x)
        p = jnp.dot(opmat[...], hi, preferred_element_type=F32)
        q = jnp.dot(opmat[0:high], lo, preferred_element_type=F32)
        added = p[0:high] + (p[high : 2 * high] + q)
        mixed = x + added[0:rows]
        flux_now = jnp.tanh(added[rows : rows + 8])
        for i, b in enumerate(spots):
            cols = slice(b * LANES, (b + 1) * LANES)
            part = slice(i * LANES, (i + 1) * LANES)
            s = flux_now[:, part]
            surf[b] = s
            for k in range(fields):
                base = k * lev
                out[base : base + lev - 8, cols] = mixed[base : base + lev - 8, part]
                moved = pltpu.roll(s, 7 - k, 0)
                low = iota((8, LANES), 0) == 7
                out[base + lev - 8 : base + lev, cols] = mixed[base + lev - 8 : base + lev, part] - jnp.where(
                    low, half * moved, 0.0
                )

    loads[2].wait()
    for i in range(groups):
        x = f[8 * i : 8 * i + 8, LANES : LANES + cells]
        y = stencil(x, i)
        out[8 * i : 8 * i + 8, LANES : cells - LANES] = y[:, LANES : cells - LANES]
    for j in range(LANES, cells - LANES, 2 * LANES):
        mix(out[:, j : j + 2 * LANES], (j // LANES, j // LANES + 1))

    to_right.wait()
    to_left.wait()
    hl = halo[0]
    hr = halo[1]
    for i in range(groups):
        s = slice(8 * i, 8 * i + 8)
        f[s, 0:LANES] = pltpu.roll(hl, LANES - 2 * i - 2, 1)
        f[s, LANES + cells : 2 * LANES + cells] = pltpu.roll(hr, LANES - 2 * i, 1) if i else hr
    lefts, rights = [], []
    for i in range(groups):
        s = slice(8 * i, 8 * i + 8)
        lefts.append(stencil(f[s, 0 : 3 * LANES], i)[:, LANES : 2 * LANES])
        rights.append(stencil(f[s, cells - LANES : cells + 2 * LANES], i)[:, LANES : 2 * LANES])
    edge = jnp.concatenate([jnp.concatenate(lefts, axis=0), jnp.concatenate(rights, axis=0)], axis=1)
    mix(edge, (0, ntile - 1))

    loads[6].wait()
    loads[7].wait()
    loads[8].wait()
    loads[9].wait()
    loads[10].wait()

    @pl.when(is_atmos)
    def _():
        for n in range(nb):
            picked = surf[ablk_s[n]].astype(BF16)
            part = jnp.dot(picked, w_v[n], preferred_element_type=F32)
            contrib[pl.ds(n, fields, stride=nb), :] = part[0:fields]
        place = toff_v[...] * oblocks + oblk_v[...]
        onehot = (iota((SPREAD * oblocks, nb), 0) == jnp.broadcast_to(place, (SPREAD * oblocks, nb))).astype(F32)
        onehot = onehot.astype(BF16)
        hi, lo = split2(contrib[...])
        for k in range(fields):
            r = slice(nb * k, nb * k + nb)
            got = jnp.dot(onehot, hi[r], preferred_element_type=F32) + jnp.dot(
                onehot, lo[r], preferred_element_type=F32
            )
            dense[:, k * LANES : (k + 1) * LANES] = got
        sends = []
        for d in range(SPREAD):
            who = lax.rem(t + d - REACH + tiles, tiles)
            send = pltpu.make_async_remote_copy(
                src_ref=dense.at[pl.ds(d * oblocks, oblocks)],
                dst_ref=recv.at[c * SPREAD + d],
                send_sem=dense_send.at[d],
                recv_sem=dense_recv.at[c * SPREAD + d],
                device_id=(ocean_row, who),
                device_id_type=MESH,
            )
            send.start()
            sends.append(send)
        for send in sends:
            send.wait_send()

    @pl.when(is_ocean)
    def _():
        total = None
        for slot in range((comps - 1) * SPREAD):
            pltpu.make_async_remote_copy(
                src_ref=dense.at[pl.ds(0, oblocks)],
                dst_ref=recv.at[slot],
                send_sem=dense_send.at[0],
                recv_sem=dense_recv.at[slot],
                device_id=(c, t),
                device_id_type=MESH,
            ).wait_recv()
            total = recv[slot] if total is None else total + recv[slot]
        land = mask_v[...].astype(F32)
        rx[...] = total * jnp.concatenate([land] * fields, axis=1)
        for k in range(fields):
            for o in range(oblocks):
                cols = slice(o * LANES, (o + 1) * LANES)
                out[k * lev : k * lev + 1, cols] += rx[o : o + 1, k * LANES : (k + 1) * LANES]


def solution(mesh):
    comps, tiles = mesh.shape["comp"], mesh.shape["tile"]

    def local(column_state, mixing, vertical, flux_coef, atm_block, ocean_block, tile_offset, remap_weights, ocean_mask):
        fields, lev, cells = column_state.shape[2:]
        nb = remap_weights.shape[2]
        rows = fields * lev
        oblocks = cells // LANES
        dims = (fields, lev, cells, comps, tiles, nb)
        result = pl.pallas_call(
            functools.partial(kernel, dims),
            out_shape=jax.ShapeDtypeStruct((rows, cells), F32),
            in_specs=[pl.BlockSpec(memory_space=pl.ANY)] * 9,
            out_specs=pl.BlockSpec(memory_space=pltpu.VMEM),
            scratch_shapes=[
                pltpu.VMEM((rows, cells + 2 * LANES), F32),
                pltpu.VMEM(mixing.shape, F32),
                pltpu.VMEM(vertical.shape, F32),
                pltpu.VMEM(flux_coef.shape, F32),
                pltpu.SMEM((nb,), jnp.int32),
                pltpu.VMEM((1, nb), jnp.int32),
                pltpu.VMEM((1, nb), jnp.int32),
                pltpu.VMEM((nb, LANES, LANES), BF16),
                pltpu.VMEM((oblocks, LANES), jnp.int32),
                pltpu.VMEM((3, rows, LANES), F32),
                pltpu.VMEM((2 * (rows + SURF), rows), BF16),
                pltpu.VMEM((2, 8, LANES), F32),
                pltpu.VMEM((2, 8, LANES), F32),
                pltpu.VMEM((oblocks, 8, LANES), F32),
                pltpu.VMEM((fields * nb, LANES), F32),
                pltpu.VMEM((SPREAD * oblocks, fields * LANES), F32),
                pltpu.VMEM(((comps - 1) * SPREAD, oblocks, fields * LANES), F32),
                pltpu.VMEM((oblocks, fields * LANES), F32),
                pltpu.SemaphoreType.DMA((11,)),
                pltpu.SemaphoreType.DMA((2,)),
                pltpu.SemaphoreType.DMA((2,)),
                pltpu.SemaphoreType.DMA((SPREAD,)),
                pltpu.SemaphoreType.DMA(((comps - 1) * SPREAD,)),
            ],
            compiler_params=pltpu.CompilerParams(collective_id=0, has_side_effects=True),
            name="step",
        )(
            column_state.reshape(rows, cells),
            mixing,
            vertical,
            flux_coef,
            atm_block.reshape(nb),
            ocean_block.reshape(1, nb),
            tile_offset.reshape(1, nb),
            remap_weights.reshape(remap_weights.shape[2:]),
            ocean_mask.reshape(oblocks, LANES),
        )
        return result.reshape(column_state.shape)

    placed = (
        P("comp", "tile", None, None, None),
        P(),
        P(),
        P(),
        P("comp", "tile", None),
        P("comp", "tile", None),
        P("comp", "tile", None),
        P("comp", "tile", None, None, None),
        P("tile", None),
    )
    return jax.shard_map(
        local,
        mesh=mesh,
        in_specs=placed,
        out_specs=P("comp", "tile", None, None, None),
        check_vma=False,
    )
```

```python
import functools

import jax
import jax.numpy as jnp
from jax import lax
from jax.experimental import pallas as pl
from jax.experimental.pallas import tpu as pltpu
from jax.sharding import PartitionSpec as P

REACH = 3
SPREAD = 2 * REACH + 1
MESH = pl.DeviceIdType.MESH
F32 = jnp.float32
BF16 = jnp.bfloat16
GREET = (-3, -1, 1, 3)
LANES = 128
SURF = 16


def iota(shape, dim):
    return lax.broadcasted_iota(jnp.int32, shape, dim)


def column(row, count):
    wide = jnp.broadcast_to(row, (count, row.shape[1]))
    keep = iota(wide.shape, 0) == iota(wide.shape, 1)
    return jnp.sum(jnp.where(keep, wide, 0.0), axis=1, keepdims=True)


def split2(x):
    hi = x.astype(BF16)
    lo = (x - hi.astype(F32)).astype(BF16)
    return hi, lo


def kernel(
    dims,
    state,
    mixing,
    vertical,
    flux,
    ablk,
    oblk,
    toff,
    weights,
    mask,
    out,
    f,
    mix_v,
    ver_v,
    flux_v,
    ablk_s,
    oblk_v,
    toff_v,
    w_v,
    mask_v,
    coef,
    opmat,
    pack,
    halo,
    surf,
    contrib,
    dense,
    recv,
    rx,
    load_sem,
    halo_send,
    halo_recv,
    dense_send,
    dense_recv,
):
    fields, lev, cells, comps, tiles, nb = dims
    rows = fields * lev
    ntile = cells // LANES
    oblocks = cells // LANES
    c = lax.axis_index("comp")
    t = lax.axis_index("tile")
    ocean_row = comps - 1
    is_atmos = c < ocean_row
    is_ocean = c == ocean_row
    group = jnp.where(is_atmos, 0, 1)
    left = lax.rem(t + tiles - 1, tiles)
    right = lax.rem(t + 1, tiles)

    loads = [
        pltpu.make_async_copy(state.at[:, pl.ds(0, LANES)], f.at[:, pl.ds(LANES, LANES)], load_sem.at[0]),
        pltpu.make_async_copy(
            state.at[:, pl.ds(cells - LANES, LANES)], f.at[:, pl.ds(cells, LANES)], load_sem.at[1]
        ),
        pltpu.make_async_copy(
            state.at[:, pl.ds(LANES, cells - 2 * LANES)],
            f.at[:, pl.ds(2 * LANES, cells - 2 * LANES)],
            load_sem.at[2],
        ),
        pltpu.make_async_copy(mixing, mix_v, load_sem.at[3]),
        pltpu.make_async_copy(vertical, ver_v, load_sem.at[4]),
        pltpu.make_async_copy(flux, flux_v, load_sem.at[5]),
        pltpu.make_async_copy(ablk, ablk_s, load_sem.at[6]),
        pltpu.make_async_copy(oblk, oblk_v, load_sem.at[7]),
        pltpu.make_async_copy(toff, toff_v, load_sem.at[8]),
        pltpu.make_async_copy(weights, w_v, load_sem.at[9]),
        pltpu.make_async_copy(mask, mask_v, load_sem.at[10]),
    ]
    barrier = pltpu.get_barrier_semaphore()
    for who in (left, right):
        pl.semaphore_signal(barrier, inc=1, device_id=(c, who), device_id_type=MESH)
    for load in loads:
        load.start()

    @pl.when(is_ocean)
    def _():
        for src in range(comps - 1):
            for d in GREET:
                who = lax.rem(t - d + tiles, tiles)
                pl.semaphore_signal(barrier, inc=1, device_id=(src, who), device_id_type=MESH)

    loads[0].wait()
    loads[1].wait()
    lane = iota((8, LANES), 1)
    groups = rows // 8
    first = jnp.zeros((8, LANES), F32)
    last = jnp.zeros((8, LANES), F32)
    for i in range(groups):
        here = lane // 2 == i
        a = f[8 * i : 8 * i + 8, LANES : 2 * LANES]
        b = f[8 * i : 8 * i + 8, cells : cells + LANES]
        first = jnp.where(here, pltpu.roll(a, 2 * i, 1) if i else a, first)
        last = jnp.where(here, pltpu.roll(b, 2 * i + 2, 1), last)
    pack[0] = first
    pack[1] = last

    loads[3].wait()
    loads[4].wait()
    loads[5].wait()
    mix_g = mix_v[group]
    rates = jnp.concatenate([column(mix_g[k : k + 1, :], lev) for k in range(fields)], axis=0)
    keep = 1.0 - 2.0 * rates
    coef[0] = jnp.broadcast_to(keep * keep + 2.0 * rates * rates, (rows, LANES))
    coef[1] = jnp.broadcast_to(2.0 * rates * keep, (rows, LANES))
    coef[2] = jnp.broadcast_to(rates * rates, (rows, LANES))
    ver_g = ver_v[group]
    spread_l = (lax.rem(iota((rows, lev), 0), lev) == iota((rows, lev), 1)).astype(F32)
    spread_r = (lax.rem(iota((lev, rows), 1), lev) == iota((lev, rows), 0)).astype(F32)
    hp = lax.Precision.HIGHEST
    tall = jnp.dot(spread_l, ver_g, precision=hp, preferred_element_type=F32)
    square = jnp.dot(tall, spread_r, precision=hp, preferred_element_type=F32)
    square = jnp.where(iota((rows, rows), 0) // lev == iota((rows, rows), 1) // lev, square, 0.0)
    fa = jnp.concatenate([column(flux_v[0:1, :], fields), jnp.zeros((SURF - fields, 1), F32)], axis=0)
    fb = jnp.concatenate([column(flux_v[1:2, :], fields), jnp.zeros((SURF - fields, 1), F32)], axis=0)
    who_row, who_col = iota((SURF, rows), 0), iota((SURF, rows), 1)
    pick = jnp.where(who_col == who_row * lev + lev - 1, fa, 0.0) + jnp.where(
        who_col == who_row * lev + lev - 2, fb, 0.0
    )
    linear = pick + jnp.dot(pick, square, precision=hp, preferred_element_type=F32)
    high = rows + SURF
    sq_hi, sq_lo = split2(jnp.concatenate([square, linear], axis=0))
    opmat[0:high] = sq_hi
    opmat[high : 2 * high] = sq_lo
    half = jnp.where(is_atmos, 0.5, 0.0)

    def stencil(x, i):
        n = x.shape[1]
        s = slice(8 * i, 8 * i + 8)
        wide = lambda v: jnp.concatenate([v] * (n // LANES), axis=1)
        near = pltpu.roll(x, 1, 1) + pltpu.roll(x, n - 1, 1)
        far = pltpu.roll(x, 2, 1) + pltpu.roll(x, n - 2, 1)
        return wide(coef[0, s]) * x + wide(coef[1, s]) * near + wide(coef[2, s]) * far

    def mix(x, spots):
        hi, lo = split2(x)
        p = jnp.dot(opmat[...], hi, preferred_element_type=F32)
        q = jnp.dot(opmat[0:high], lo, preferred_element_type=F32)
        added = p[0:high] + (p[high : 2 * high] + q)
        mixed = x + added[0:rows]
        flux_now = jnp.tanh(added[rows : rows + 8])
        for i, b in enumerate(spots):
            cols = slice(b * LANES, (b + 1) * LANES)
            part = slice(i * LANES, (i + 1) * LANES)
            s = flux_now[:, part]
            surf[b] = s
            for k in range(fields):
                base = k * lev
                out[base : base + lev - 8, cols] = mixed[base : base + lev - 8, part]
                moved = pltpu.roll(s, 7 - k, 0)
                low = iota((8, LANES), 0) == 7
                out[base + lev - 8 : base + lev, cols] = mixed[base + lev - 8 : base + lev, part] - jnp.where(
                    low, half * moved, 0.0
                )

    loads[2].wait()
    for i in range(groups):
        x = f[8 * i : 8 * i + 8, LANES : LANES + cells]
        y = stencil(x, i)
        out[8 * i : 8 * i + 8, LANES : cells - LANES] = y[:, LANES : cells - LANES]
    pl.semaphore_wait(barrier, jnp.where(is_atmos, 2 + len(GREET), 2))
    to_right = pltpu.make_async_remote_copy(
        src_ref=pack.at[1],
        dst_ref=halo.at[0],
        send_sem=halo_send.at[0],
        recv_sem=halo_recv.at[0],
        device_id=(c, right),
        device_id_type=MESH,
    )
    to_left = pltpu.make_async_remote_copy(
        src_ref=pack.at[0],
        dst_ref=halo.at[1],
        send_sem=halo_send.at[1],
        recv_sem=halo_recv.at[1],
        device_id=(c, left),
        device_id_type=MESH,
    )
    to_right.start()
    to_left.start()

    for j in range(LANES, cells - LANES, 2 * LANES):
        mix(out[:, j : j + 2 * LANES], (j // LANES, j // LANES + 1))

    to_right.wait()
    to_left.wait()
    hl = halo[0]
    hr = halo[1]
    for i in range(groups):
        s = slice(8 * i, 8 * i + 8)
        f[s, 0:LANES] = pltpu.roll(hl, LANES - 2 * i - 2, 1)
        f[s, LANES + cells : 2 * LANES + cells] = pltpu.roll(hr, LANES - 2 * i, 1) if i else hr
    lefts, rights = [], []
    for i in range(groups):
        s = slice(8 * i, 8 * i + 8)
        lefts.append(stencil(f[s, 0 : 3 * LANES], i)[:, LANES : 2 * LANES])
        rights.append(stencil(f[s, cells - LANES : cells + 2 * LANES], i)[:, LANES : 2 * LANES])
    edge = jnp.concatenate([jnp.concatenate(lefts, axis=0), jnp.concatenate(rights, axis=0)], axis=1)
    mix(edge, (0, ntile - 1))

    loads[6].wait()
    loads[7].wait()
    loads[8].wait()
    loads[9].wait()
    loads[10].wait()

    @pl.when(is_atmos)
    def _():
        for n in range(nb):
            picked = surf[ablk_s[n]].astype(BF16)
            part = jnp.dot(picked, w_v[n], preferred_element_type=F32)
            contrib[pl.ds(n, fields, stride=nb), :] = part[0:fields]
        place = toff_v[...] * oblocks + oblk_v[...]
        onehot = (iota((SPREAD * oblocks, nb), 0) == jnp.broadcast_to(place, (SPREAD * oblocks, nb))).astype(F32)
        onehot = onehot.astype(BF16)
        hi, lo = split2(contrib[...])
        for k in range(fields):
            r = slice(nb * k, nb * k + nb)
            got = jnp.dot(onehot, hi[r], preferred_element_type=F32) + jnp.dot(
                onehot, lo[r], preferred_element_type=F32
            )
            dense[:, k * LANES : (k + 1) * LANES] = got
        spin = lax.rem(t, 4)
        sends = []
        for step in range(SPREAD):
            if step < REACH:
                d = REACH + 1 + lax.rem(step + 2 * REACH - spin, REACH)
            else:
                d = SPREAD - 1 - step
            who = lax.rem(t + d - REACH + tiles, tiles)
            send = pltpu.make_async_remote_copy(
                src_ref=dense.at[pl.ds(d * oblocks, oblocks)],
                dst_ref=recv.at[c * SPREAD + d],
                send_sem=dense_send.at[step],
                recv_sem=dense_recv.at[c * SPREAD + d],
                device_id=(ocean_row, who),
                device_id_type=MESH,
            )
            send.start()
            sends.append(send)
        for send in sends:
            send.wait_send()

    @pl.when(is_ocean)
    def _():
        total = None
        for slot in sorted(range((comps - 1) * SPREAD), key=lambda slot: slot % SPREAD):
            pltpu.make_async_remote_copy(
                src_ref=dense.at[pl.ds(0, oblocks)],
                dst_ref=recv.at[slot],
                send_sem=dense_send.at[0],
                recv_sem=dense_recv.at[slot],
                device_id=(c, t),
                device_id_type=MESH,
            ).wait_recv()
            total = recv[slot] if total is None else total + recv[slot]
        land = mask_v[...].astype(F32)
        rx[...] = total * jnp.concatenate([land] * fields, axis=1)
        for k in range(fields):
            for o in range(oblocks):
                cols = slice(o * LANES, (o + 1) * LANES)
                out[k * lev : k * lev + 1, cols] += rx[o : o + 1, k * LANES : (k + 1) * LANES]


def solution(mesh):
    comps, tiles = mesh.shape["comp"], mesh.shape["tile"]

    def local(column_state, mixing, vertical, flux_coef, atm_block, ocean_block, tile_offset, remap_weights, ocean_mask):
        fields, lev, cells = column_state.shape[2:]
        nb = remap_weights.shape[2]
        rows = fields * lev
        oblocks = cells // LANES
        dims = (fields, lev, cells, comps, tiles, nb)
        result = pl.pallas_call(
            functools.partial(kernel, dims),
            out_shape=pltpu.VMEM((rows, cells), F32),
            in_specs=[pl.BlockSpec(memory_space=pl.ANY)] * 9,
            out_specs=pl.BlockSpec(memory_space=pltpu.VMEM),
            scratch_shapes=[
                pltpu.VMEM((rows, cells + 2 * LANES), F32),
                pltpu.VMEM(mixing.shape, F32),
                pltpu.VMEM(vertical.shape, F32),
                pltpu.VMEM(flux_coef.shape, F32),
                pltpu.SMEM((nb,), jnp.int32),
                pltpu.VMEM((1, nb), jnp.int32),
                pltpu.VMEM((1, nb), jnp.int32),
                pltpu.VMEM((nb, LANES, LANES), BF16),
                pltpu.VMEM((oblocks, LANES), jnp.int32),
                pltpu.VMEM((3, rows, LANES), F32),
                pltpu.VMEM((2 * (rows + SURF), rows), BF16),
                pltpu.VMEM((2, 8, LANES), F32),
                pltpu.VMEM((2, 8, LANES), F32),
                pltpu.VMEM((oblocks, 8, LANES), F32),
                pltpu.VMEM((fields * nb, LANES), F32),
                pltpu.VMEM((SPREAD * oblocks, fields * LANES), F32),
                pltpu.VMEM(((comps - 1) * SPREAD, oblocks, fields * LANES), F32),
                pltpu.VMEM((oblocks, fields * LANES), F32),
                pltpu.SemaphoreType.DMA((11,)),
                pltpu.SemaphoreType.DMA((2,)),
                pltpu.SemaphoreType.DMA((2,)),
                pltpu.SemaphoreType.DMA((SPREAD,)),
                pltpu.SemaphoreType.DMA(((comps - 1) * SPREAD,)),
            ],
            compiler_params=pltpu.CompilerParams(collective_id=0, has_side_effects=True),
            name="step",
        )(
            column_state.reshape(rows, cells),
            mixing,
            vertical,
            flux_coef,
            atm_block.reshape(nb),
            ocean_block.reshape(1, nb),
            tile_offset.reshape(1, nb),
            remap_weights.reshape(remap_weights.shape[2:]),
            ocean_mask.reshape(oblocks, LANES),
        )
        return result.reshape(column_state.shape)

    placed = (
        P("comp", "tile", None, None, None),
        P(),
        P(),
        P(),
        P("comp", "tile", None),
        P("comp", "tile", None),
        P("comp", "tile", None),
        P("comp", "tile", None, None, None),
        P("tile", None),
    )
    return jax.shard_map(
        local,
        mesh=mesh,
        in_specs=placed,
        out_specs=P("comp", "tile", None, None, None),
        check_vma=False,
    )
```

```python
import functools

import jax
import jax.numpy as jnp
from jax import lax
from jax.experimental import pallas as pl
from jax.experimental.pallas import tpu as pltpu
from jax.sharding import PartitionSpec as P

REACH = 3
SPREAD = 2 * REACH + 1
MESH = pl.DeviceIdType.MESH
F32 = jnp.float32
BF16 = jnp.bfloat16
HALF = 4
PLANE = 8
LANES = 128
SURF = 16
GROUP = 16


def iota(shape, dim):
    return lax.broadcasted_iota(jnp.int32, shape, dim)


def column(row, count):
    wide = jnp.broadcast_to(row, (count, row.shape[1]))
    keep = iota(wide.shape, 0) == iota(wide.shape, 1)
    return jnp.sum(jnp.where(keep, wide, 0.0), axis=1, keepdims=True)


def split2(x):
    hi = x.astype(BF16)
    lo = (x - hi.astype(F32)).astype(BF16)
    return hi, lo


def kernel(
    dims,
    state,
    mixing,
    vertical,
    flux,
    ablk,
    oblk,
    toff,
    weights,
    mask,
    out,
    f,
    mix_v,
    ver_v,
    flux_v,
    ablk_s,
    oblk_v,
    toff_v,
    w_v,
    mask_v,
    coef,
    opmat,
    pack,
    halo,
    surf,
    contrib,
    dense,
    recv,
    relay,
    packed_ops,
    rx,
    load_sem,
    halo_send,
    halo_recv,
    relay_send,
    relay_recv,
    dense_send,
    dense_recv,
    known,
):
    fields, lev, cells, comps, tiles, nb = dims
    rows = fields * lev
    ntile = cells // LANES
    oblocks = cells // LANES
    c = lax.axis_index("comp")
    t = lax.axis_index("tile")
    ocean_row = comps - 1
    is_atmos = c < ocean_row
    is_ocean = c == ocean_row
    group = jnp.where(is_atmos, 0, 1)
    left = lax.rem(t + tiles - 1, tiles)
    right = lax.rem(t + 1, tiles)

    loads = [
        pltpu.make_async_copy(state.at[:, pl.ds(0, LANES)], f.at[:, pl.ds(LANES, LANES)], load_sem.at[0]),
        pltpu.make_async_copy(
            state.at[:, pl.ds(cells - LANES, LANES)], f.at[:, pl.ds(cells, LANES)], load_sem.at[1]
        ),
        pltpu.make_async_copy(
            state.at[:, pl.ds(LANES, cells - 2 * LANES)],
            f.at[:, pl.ds(2 * LANES, cells - 2 * LANES)],
            load_sem.at[2],
        ),
        pltpu.make_async_copy(mixing, mix_v, load_sem.at[3]),
        pltpu.make_async_copy(vertical, ver_v, load_sem.at[4]),
        pltpu.make_async_copy(flux, flux_v, load_sem.at[5]),
        pltpu.make_async_copy(ablk, ablk_s, load_sem.at[6]),
        pltpu.make_async_copy(oblk, oblk_v, load_sem.at[7]),
        pltpu.make_async_copy(toff, toff_v, load_sem.at[8]),
        pltpu.make_async_copy(weights, w_v, load_sem.at[9]),
        pltpu.make_async_copy(mask, mask_v, load_sem.at[10]),
    ]
    barrier = pltpu.get_barrier_semaphore()
    spot = lax.rem(t, PLANE)
    first_spot = spot == 0
    last_spot = spot == PLANE - 1

    def greet(row, who):
        pl.semaphore_signal(barrier, inc=1, device_id=(row, lax.rem(who + tiles, tiles)), device_id_type=MESH)

    greet(c, t - 1)

    @pl.when(jnp.logical_not(last_spot))
    def _():
        greet(c, t + 1)

    @pl.when(last_spot)
    def _():
        greet(c, t + PLANE)
        greet(c, t - PLANE + 1)

    for load in loads:
        load.start()

    @pl.when(is_atmos)
    def _():
        for d in range(1, REACH + 1):

            @pl.when(spot < d)
            def _():
                greet(ocean_row, t - d)

    @pl.when(is_ocean)
    def _():
        for d in range(-REACH, REACH + 1):
            there = spot - d
            wanted = (there < HALF) & (there >= 0) if d else spot < PLANE
            if d > 0:
                wanted = wanted | (there < 0)

            @pl.when(wanted)
            def _():
                for src in range(comps - 1):
                    greet(src, t - d)

    loads[0].wait()
    loads[1].wait()
    lane = iota((8, LANES), 1)
    sub = iota((8, LANES), 0)
    place_in = lane % GROUP
    groups = rows // 8
    packed = jnp.zeros((8, LANES), F32)
    for i in range(groups):
        here = lane // GROUP == i
        a = f[8 * i : 8 * i + 8, LANES : 2 * LANES]
        b = f[8 * i : 8 * i + 8, cells : cells + LANES]
        packed = jnp.where(here & (place_in < 7), pltpu.roll(a, GROUP * i + 2, 1), packed)
        packed = jnp.where(here & (place_in >= 7), pltpu.roll(b, (GROUP * i + 12) % LANES, 1), packed)
    pack[...] = packed

    loads[3].wait()
    loads[4].wait()
    loads[5].wait()
    def rate_column(mix_g):
        return jnp.concatenate([column(mix_g[k : k + 1, :], lev) for k in range(fields)], axis=0)

    rates = rate_column(mix_v[group])
    keep = 1.0 - 2.0 * rates
    coef[0] = jnp.broadcast_to(keep * keep + 2.0 * rates * rates, (rows, LANES))
    coef[1] = jnp.broadcast_to(2.0 * rates * keep, (rows, LANES))
    coef[2] = jnp.broadcast_to(rates * rates, (rows, LANES))
    spread = (lax.rem(iota((lev, rows), 1), lev) == iota((lev, rows), 0)).astype(F32)
    stacked = jnp.concatenate([ver_v[group]] * fields + [ver_v[group][lev - 8 : lev]], axis=0)
    wide = jnp.dot(stacked, spread, precision=lax.Precision.HIGHEST, preferred_element_type=F32)
    square = jnp.where(iota((rows, rows), 0) // lev == iota((rows, rows), 1) // lev, wide[0:rows], 0.0)
    fa = jnp.concatenate([column(flux_v[0:1, :], fields), jnp.zeros((SURF - fields, 1), F32)], axis=0)
    fb = jnp.concatenate([column(flux_v[1:2, :], fields), jnp.zeros((SURF - fields, 1), F32)], axis=0)
    who_row, who_col = iota((SURF, rows), 0), iota((SURF, rows), 1)
    level = who_col % lev
    top = jnp.where(level == lev - 1, 1.0, 0.0) + wide[rows + 7 : rows + 8]
    under = jnp.where(level == lev - 2, 1.0, 0.0) + wide[rows + 6 : rows + 7]
    linear = jnp.where(who_col // lev == who_row, fa * top + fb * under, 0.0)
    high = rows + SURF
    sq_hi, sq_lo = split2(jnp.concatenate([square, linear], axis=0))
    opmat[0:high] = sq_hi
    opmat[high : 2 * high] = sq_lo
    half = jnp.where(is_atmos, 0.5, 0.0)

    def packed_column(v):
        got = jnp.zeros((8, LANES), F32)
        for i in range(groups):
            got = jnp.where(lane // GROUP == i, jnp.broadcast_to(v[8 * i : 8 * i + 8], (8, LANES)), got)
        return got

    pr = packed_column(rates)
    pk = 1.0 - 2.0 * pr
    lin = packed_column(column(jnp.sum(linear, axis=0, keepdims=True), rows))
    packed_ops[0] = pk * pk + 2.0 * pr * pr
    packed_ops[1] = 2.0 * pr * pk
    packed_ops[2] = pr * pr
    packed_ops[3] = lin

    def stencil(x, i):
        n = x.shape[1]
        s = slice(8 * i, 8 * i + 8)
        wide = lambda v: jnp.concatenate([v] * (n // LANES), axis=1)
        near = pltpu.roll(x, 1, 1) + pltpu.roll(x, n - 1, 1)
        far = pltpu.roll(x, 2, 1) + pltpu.roll(x, n - 2, 1)
        return wide(coef[0, s]) * x + wide(coef[1, s]) * near + wide(coef[2, s]) * far

    def mix(x, spots, store_surface):
        hi, lo = split2(x)
        p = jnp.dot(opmat[...], hi, preferred_element_type=F32)
        q = jnp.dot(opmat[0:high], lo, preferred_element_type=F32)
        added = p[0:high] + (p[high : 2 * high] + q)
        mixed = x + added[0:rows]
        flux_now = jnp.tanh(added[rows : rows + 8])
        for i, b in enumerate(spots):
            cols = slice(b * LANES, (b + 1) * LANES)
            part = slice(i * LANES, (i + 1) * LANES)
            s = flux_now[:, part]
            if store_surface:
                kept = s
                if b == 0:
                    kept = jnp.where((sub < fields) & (lane < 2), 0.0, kept)
                    kept = jnp.where((sub >= 4) & (sub < 6) & (lane == sub - 4), 1.0, kept)
                if b == ntile - 1:
                    kept = jnp.where((sub < fields) & (lane >= LANES - 2), 0.0, kept)
                    kept = jnp.where((sub >= 6) & (lane == LANES - 8 + sub), 1.0, kept)
                surf[b] = kept
            for k in range(fields):
                base = k * lev
                out[base : base + lev - 8, cols] = mixed[base : base + lev - 8, part]
                moved = pltpu.roll(s, 7 - k, 0)
                low = sub == 7
                out[base + lev - 8 : base + lev, cols] = mixed[base + lev - 8 : base + lev, part] - jnp.where(
                    low, half * moved, 0.0
                )

    loads[2].wait()
    for i in range(groups):
        s = slice(8 * i, 8 * i + 8)
        out[s, :] = stencil(f[s, LANES : LANES + cells], i)
    pl.semaphore_wait(
        barrier,
        jnp.where(last_spot, 3, 2) + jnp.where(
            is_atmos,
            jnp.where(spot < HALF, spot + 1 + REACH, 1 + jnp.maximum(spot - (PLANE - 1 - REACH), 0)),
            (comps - 1) * jnp.maximum(spot - (PLANE - 1 - REACH), 0),
        ),
    )

    def pack_copy(way, src, dst, send, recv_at, who):
        return pltpu.make_async_remote_copy(
            src_ref=src,
            dst_ref=dst,
            send_sem=send,
            recv_sem=recv_at,
            device_id=(c, lax.rem(who + tiles, tiles)),
            device_id_type=MESH,
        )

    to_right = pack_copy(0, pack, halo.at[0], halo_send.at[0], halo_recv.at[0], t + 1)
    to_left = pack_copy(1, pack, halo.at[1], halo_send.at[1], halo_recv.at[1], t - 1)
    to_relay = pack_copy(1, pack, relay, relay_send.at[0], relay_recv.at[0], t + PLANE - 1)
    onward = pack_copy(1, relay, halo.at[1], relay_send.at[1], halo_recv.at[1], t - PLANE)

    to_right.start()

    @pl.when(is_ocean)
    def _():
        for d in range(1, REACH + 1):

            @pl.when(spot + d >= PLANE)
            def _():
                for src in range(comps - 1):
                    who = (src, lax.rem(t + d, tiles))
                    pl.semaphore_signal(known.at[4], inc=1, device_id=who, device_id_type=MESH)

    @pl.when(jnp.logical_not(first_spot))
    def _():
        to_left.start()

    @pl.when(first_spot)
    def _():
        to_relay.start()

    @pl.when(last_spot)
    def _():
        to_relay.wait_recv()
        onward.start()

    for j in range(0, cells, 2 * LANES):
        mix(out[:, j : j + 2 * LANES], (j // LANES, j // LANES + 1), True)
    loads[6].wait()
    loads[7].wait()
    loads[8].wait()
    loads[9].wait()
    loads[10].wait()

    @pl.when(is_atmos)
    def _():
        for n in range(nb):
            picked = surf[ablk_s[n]].astype(BF16)
            part = jnp.dot(picked, w_v[n], preferred_element_type=F32)
            contrib[pl.ds(n, 8, stride=nb), :] = part

    to_right.wait_recv()
    to_left.wait_recv()

    def dense_copy(d):
        return pltpu.make_async_remote_copy(
            src_ref=dense.at[pl.ds((d + REACH) * oblocks, oblocks)],
            dst_ref=recv.at[c * SPREAD + d + REACH],
            send_sem=dense_send.at[d + REACH],
            recv_sem=dense_recv.at[c * SPREAD + d + REACH],
            device_id=(ocean_row, lax.rem(t + d + tiles, tiles)),
            device_id_type=MESH,
        )

    @pl.when(is_atmos)
    def _():
        x = jnp.where(place_in < 2, pltpu.roll(halo[0], LANES - 10, 1), pack[...])
        x = jnp.where(place_in >= 12, pltpu.roll(halo[1], 10, 1), x)
        near = pltpu.roll(x, 1, 1) + pltpu.roll(x, LANES - 1, 1)
        far = pltpu.roll(x, 2, 1) + pltpu.roll(x, LANES - 2, 1)
        z = packed_ops[3] * (packed_ops[0] * x + packed_ops[1] * near + packed_ops[2] * far)
        for shift in (4, 2, 1):
            z = z + pltpu.roll(z, shift, 0)
        z = z + pltpu.roll(z, LANES - GROUP, 1)
        r = jnp.tanh(z).astype(BF16).astype(F32)
        place = toff_v[...] * oblocks + oblk_v[...]
        onehot = (iota((SPREAD * oblocks, nb), 0) == jnp.broadcast_to(place, (SPREAD * oblocks, nb))).astype(F32)
        onehot = onehot.astype(BF16)
        for k in range(fields):
            got = contrib[nb * k : nb * k + nb, :]
            for e, p in enumerate((2, 3, 10, 11)):
                at = 2 * k * GROUP + p
                scale = jnp.broadcast_to(r[:, at : at + 1], (8, LANES))
                scale = jnp.concatenate([scale] * (nb // 8), axis=0)
                got = got + scale * contrib[nb * (4 + e) : nb * (5 + e), :]
            hi, lo = split2(got)
            dense[:, k * LANES : (k + 1) * LANES] = jnp.dot(onehot, hi, preferred_element_type=F32) + jnp.dot(
                onehot, lo, preferred_element_type=F32
            )
        for d in range(1, REACH + 1):

            @pl.when(spot + d >= PLANE)
            def _():
                dense_copy(d).start()

        def inside(d):
            return (spot + d >= 0) & (spot + d < PLANE)

        def send(d, wanted):
            @pl.when(wanted)
            def _():
                dense_copy(d).start()

        def tell(stage, who, wanted):
            @pl.when(wanted)
            def _():
                pl.semaphore_signal(known.at[stage], inc=1, device_id=(c, who), device_id_type=MESH)

        upper = spot >= HALF
        tell(0, right, (spot >= HALF - 1) & (spot < PLANE - 1))
        tell(1, left, (spot == HALF + 1) | (spot == HALF + 2))
        for d in (0, -1, 1):
            send(d, inside(d))
        for d in (-2, 2, -3, 3):
            send(d, inside(d) & jnp.logical_not(upper))

        @pl.when(spot < REACH)
        def _():
            pl.semaphore_wait(known.at[4], REACH - spot)
            for d in range(1, REACH + 1):
                send(-d, spot < d)

        @pl.when(upper)
        def _():
            pl.semaphore_wait(known.at[0], 1)
            tell(2, right, spot < PLANE - 1)
            dense_copy(-2).start()

            @pl.when(spot < HALF + 2)
            def _():
                pl.semaphore_wait(known.at[1], 1)
                tell(3, left, spot == HALF + 1)
                dense_copy(2).start()

            @pl.when(spot > HALF)
            def _():
                pl.semaphore_wait(known.at[2], 1)

            dense_copy(-3).start()

            @pl.when(spot == HALF)
            def _():
                pl.semaphore_wait(known.at[3], 1)
                dense_copy(3).start()

    hl = halo[0]
    hr = halo[1]
    for i in range(groups):
        s = slice(8 * i, 8 * i + 8)
        f[s, 0:LANES] = pltpu.roll(hl, (116 - GROUP * i) % LANES, 1)
        f[s, LANES + cells : 2 * LANES + cells] = pltpu.roll(hr, 126 - GROUP * i, 1)
    lefts, rights = [], []
    for i in range(groups):
        s = slice(8 * i, 8 * i + 8)
        lefts.append(stencil(f[s, 0 : 3 * LANES], i)[:, LANES : 2 * LANES])
        rights.append(stencil(f[s, cells - LANES : cells + 2 * LANES], i)[:, LANES : 2 * LANES])
    edge = jnp.concatenate([jnp.concatenate(lefts, axis=0), jnp.concatenate(rights, axis=0)], axis=1)
    mix(edge, (0, ntile - 1), False)

    to_right.wait_send()

    @pl.when(jnp.logical_not(first_spot))
    def _():
        to_left.wait_send()

    @pl.when(first_spot)
    def _():
        to_relay.wait_send()

    @pl.when(last_spot)
    def _():
        onward.wait_send()

    @pl.when(is_atmos)
    def _():
        for d in range(-REACH, REACH + 1):
            dense_copy(d).wait_send()

    @pl.when(is_ocean)
    def _():
        total = None
        for slot in sorted(range((comps - 1) * SPREAD), key=lambda slot: slot % SPREAD):
            pltpu.make_async_remote_copy(
                src_ref=dense.at[pl.ds(0, oblocks)],
                dst_ref=recv.at[slot],
                send_sem=dense_send.at[0],
                recv_sem=dense_recv.at[slot],
                device_id=(c, t),
                device_id_type=MESH,
            ).wait_recv()
            total = recv[slot] if total is None else total + recv[slot]
        land = mask_v[...].astype(F32)
        rx[...] = total * jnp.concatenate([land] * fields, axis=1)
        for k in range(fields):
            for o in range(oblocks):
                cols = slice(o * LANES, (o + 1) * LANES)
                out[k * lev : k * lev + 1, cols] += rx[o : o + 1, k * LANES : (k + 1) * LANES]


def solution(mesh):
    comps, tiles = mesh.shape["comp"], mesh.shape["tile"]

    def local(column_state, mixing, vertical, flux_coef, atm_block, ocean_block, tile_offset, remap_weights, ocean_mask):
        fields, lev, cells = column_state.shape[2:]
        nb = remap_weights.shape[2]
        rows = fields * lev
        oblocks = cells // LANES
        dims = (fields, lev, cells, comps, tiles, nb)
        result = pl.pallas_call(
            functools.partial(kernel, dims),
            out_shape=pltpu.VMEM((rows, cells), F32),
            in_specs=[pl.BlockSpec(memory_space=pl.ANY)] * 9,
            out_specs=pl.BlockSpec(memory_space=pltpu.VMEM),
            scratch_shapes=[
                pltpu.VMEM((rows, cells + 2 * LANES), F32),
                pltpu.VMEM(mixing.shape, F32),
                pltpu.VMEM(vertical.shape, F32),
                pltpu.VMEM(flux_coef.shape, F32),
                pltpu.SMEM((nb,), jnp.int32),
                pltpu.VMEM((1, nb), jnp.int32),
                pltpu.VMEM((1, nb), jnp.int32),
                pltpu.VMEM((nb, LANES, LANES), BF16),
                pltpu.VMEM((oblocks, LANES), jnp.int32),
                pltpu.VMEM((3, rows, LANES), F32),
                pltpu.VMEM((2 * (rows + SURF), rows), BF16),
                pltpu.VMEM((8, LANES), F32),
                pltpu.VMEM((2, 8, LANES), F32),
                pltpu.VMEM((oblocks, 8, LANES), F32),
                pltpu.VMEM((8 * nb, LANES), F32),
                pltpu.VMEM((SPREAD * oblocks, fields * LANES), F32),
                pltpu.VMEM(((comps - 1) * SPREAD, oblocks, fields * LANES), F32),
                pltpu.VMEM((8, LANES), F32),
                pltpu.VMEM((4, 8, LANES), F32),
                pltpu.VMEM((oblocks, fields * LANES), F32),
                pltpu.SemaphoreType.DMA((11,)),
                pltpu.SemaphoreType.DMA((2,)),
                pltpu.SemaphoreType.DMA((2,)),
                pltpu.SemaphoreType.DMA((2,)),
                pltpu.SemaphoreType.DMA((1,)),
                pltpu.SemaphoreType.DMA((SPREAD,)),
                pltpu.SemaphoreType.DMA(((comps - 1) * SPREAD,)),
                pltpu.SemaphoreType.REGULAR((5,)),
            ],
            compiler_params=pltpu.CompilerParams(collective_id=0, has_side_effects=True),
            name="step",
        )(
            column_state.reshape(rows, cells),
            mixing,
            vertical,
            flux_coef,
            atm_block.reshape(nb),
            ocean_block.reshape(1, nb),
            tile_offset.reshape(1, nb),
            remap_weights.reshape(remap_weights.shape[2:]),
            ocean_mask.reshape(oblocks, LANES),
        )
        return result.reshape(column_state.shape)

    placed = (
        P("comp", "tile", None, None, None),
        P(),
        P(),
        P(),
        P("comp", "tile", None),
        P("comp", "tile", None),
        P("comp", "tile", None),
        P("comp", "tile", None, None, None),
        P("tile", None),
    )
    return jax.shard_map(
        local,
        mesh=mesh,
        in_specs=placed,
        out_specs=P("comp", "tile", None, None, None),
        check_vma=False,
    )
```

```python
import functools

import jax
import jax.numpy as jnp
from jax import lax
from jax.experimental import pallas as pl
from jax.experimental.pallas import tpu as pltpu
from jax.sharding import PartitionSpec as P

REACH = 3
SPREAD = 2 * REACH + 1
MESH = pl.DeviceIdType.MESH
F32 = jnp.float32
BF16 = jnp.bfloat16
HALF = 4
PLANE = 8
LANES = 128
SURF = 16
GROUP = 16


def iota(shape, dim):
    return lax.broadcasted_iota(jnp.int32, shape, dim)


def column(row, count):
    wide = jnp.broadcast_to(row, (count, row.shape[1]))
    keep = iota(wide.shape, 0) == iota(wide.shape, 1)
    return jnp.sum(jnp.where(keep, wide, 0.0), axis=1, keepdims=True)


def split2(x):
    hi = x.astype(BF16)
    lo = (x - hi.astype(F32)).astype(BF16)
    return hi, lo


def kernel(
    dims,
    state,
    mixing,
    vertical,
    flux,
    ablk,
    oblk,
    toff,
    weights,
    mask,
    out,
    f,
    mix_v,
    ver_v,
    flux_v,
    ablk_s,
    oblk_v,
    toff_v,
    w_v,
    mask_v,
    coef,
    opmat,
    pack,
    halo,
    surf,
    contrib,
    dense,
    recv,
    relay,
    packed_ops,
    rx,
    load_sem,
    halo_send,
    halo_recv,
    relay_send,
    relay_recv,
    dense_send,
    dense_recv,
    known,
):
    fields, lev, cells, comps, tiles, nb = dims
    rows = fields * lev
    ntile = cells // LANES
    oblocks = cells // LANES
    c = lax.axis_index("comp")
    t = lax.axis_index("tile")
    ocean_row = comps - 1
    is_atmos = c < ocean_row
    is_ocean = c == ocean_row
    group = jnp.where(is_atmos, 0, 1)
    left = lax.rem(t + tiles - 1, tiles)
    right = lax.rem(t + 1, tiles)

    loads = [
        pltpu.make_async_copy(state.at[:, pl.ds(0, LANES)], f.at[:, pl.ds(LANES, LANES)], load_sem.at[0]),
        pltpu.make_async_copy(
            state.at[:, pl.ds(cells - LANES, LANES)], f.at[:, pl.ds(cells, LANES)], load_sem.at[1]
        ),
        pltpu.make_async_copy(
            state.at[:, pl.ds(LANES, cells - 2 * LANES)],
            f.at[:, pl.ds(2 * LANES, cells - 2 * LANES)],
            load_sem.at[2],
        ),
        pltpu.make_async_copy(mixing, mix_v, load_sem.at[3]),
        pltpu.make_async_copy(vertical, ver_v, load_sem.at[4]),
        pltpu.make_async_copy(flux, flux_v, load_sem.at[5]),
        pltpu.make_async_copy(ablk, ablk_s, load_sem.at[6]),
        pltpu.make_async_copy(oblk, oblk_v, load_sem.at[7]),
        pltpu.make_async_copy(toff, toff_v, load_sem.at[8]),
        pltpu.make_async_copy(weights, w_v, load_sem.at[9]),
        pltpu.make_async_copy(mask, mask_v, load_sem.at[10]),
    ]
    barrier = pltpu.get_barrier_semaphore()
    spot = lax.rem(t, PLANE)
    start = t == 0
    helper = t == PLANE - 1
    end = t == tiles - 1

    def greet(row, who):
        pl.semaphore_signal(barrier, inc=1, device_id=(row, lax.rem(who + tiles, tiles)), device_id_type=MESH)

    greet(c, t - 1)

    greet(c, jnp.where(end, t + PLANE, t + 1))

    @pl.when(helper)
    def _():
        greet(c, t - PLANE + 1)

    for load in loads:
        load.start()

    @pl.when(is_atmos)
    def _():
        for d in range(1, REACH + 1):

            @pl.when(spot < d)
            def _():
                greet(ocean_row, t - d)

    @pl.when(is_ocean)
    def _():
        for d in range(-REACH, REACH + 1):
            there = spot - d
            wanted = (there < HALF) & (there >= 0) if d else spot < PLANE
            if d > 0:
                wanted = wanted | (there < 0)

            @pl.when(wanted)
            def _():
                for src in range(comps - 1):
                    greet(src, t - d)

    loads[0].wait()
    loads[1].wait()
    lane = iota((8, LANES), 1)
    sub = iota((8, LANES), 0)
    place_in = lane % GROUP
    groups = rows // 8
    packed = jnp.zeros((8, LANES), F32)
    for i in range(groups):
        here = lane // GROUP == i
        a = f[8 * i : 8 * i + 8, LANES : 2 * LANES]
        b = f[8 * i : 8 * i + 8, cells : cells + LANES]
        packed = jnp.where(here & (place_in < 7), pltpu.roll(a, GROUP * i + 2, 1), packed)
        packed = jnp.where(here & (place_in >= 7), pltpu.roll(b, (GROUP * i + 12) % LANES, 1), packed)
    pack[...] = packed

    loads[3].wait()
    loads[4].wait()
    loads[5].wait()
    def rate_column(mix_g):
        return jnp.concatenate([column(mix_g[k : k + 1, :], lev) for k in range(fields)], axis=0)

    rates = rate_column(mix_v[group])
    keep = 1.0 - 2.0 * rates
    coef[0] = jnp.broadcast_to(keep * keep + 2.0 * rates * rates, (rows, LANES))
    coef[1] = jnp.broadcast_to(2.0 * rates * keep, (rows, LANES))
    coef[2] = jnp.broadcast_to(rates * rates, (rows, LANES))
    spread = (lax.rem(iota((lev, rows), 1), lev) == iota((lev, rows), 0)).astype(F32)
    stacked = jnp.concatenate([ver_v[group]] * fields + [ver_v[group][lev - 8 : lev]], axis=0)
    wide = jnp.dot(stacked, spread, precision=lax.Precision.HIGHEST, preferred_element_type=F32)
    square = jnp.where(iota((rows, rows), 0) // lev == iota((rows, rows), 1) // lev, wide[0:rows], 0.0)
    fa = jnp.concatenate([column(flux_v[0:1, :], fields), jnp.zeros((SURF - fields, 1), F32)], axis=0)
    fb = jnp.concatenate([column(flux_v[1:2, :], fields), jnp.zeros((SURF - fields, 1), F32)], axis=0)
    who_row, who_col = iota((SURF, rows), 0), iota((SURF, rows), 1)
    level = who_col % lev
    top = jnp.where(level == lev - 1, 1.0, 0.0) + wide[rows + 7 : rows + 8]
    under = jnp.where(level == lev - 2, 1.0, 0.0) + wide[rows + 6 : rows + 7]
    linear = jnp.where(who_col // lev == who_row, fa * top + fb * under, 0.0)
    high = rows + SURF
    sq_hi, sq_lo = split2(jnp.concatenate([square, linear], axis=0))
    opmat[0:high] = sq_hi
    opmat[high : 2 * high] = sq_lo
    half = jnp.where(is_atmos, 0.5, 0.0)

    def packed_column(v):
        got = jnp.zeros((8, LANES), F32)
        for i in range(groups):
            got = jnp.where(lane // GROUP == i, jnp.broadcast_to(v[8 * i : 8 * i + 8], (8, LANES)), got)
        return got

    pr = packed_column(rates)
    pk = 1.0 - 2.0 * pr
    lin = packed_column(column(jnp.sum(linear, axis=0, keepdims=True), rows))
    packed_ops[0] = pk * pk + 2.0 * pr * pr
    packed_ops[1] = 2.0 * pr * pk
    packed_ops[2] = pr * pr
    packed_ops[3] = lin

    def stencil(x, i):
        n = x.shape[1]
        s = slice(8 * i, 8 * i + 8)
        wide = lambda v: jnp.concatenate([v] * (n // LANES), axis=1)
        near = pltpu.roll(x, 1, 1) + pltpu.roll(x, n - 1, 1)
        far = pltpu.roll(x, 2, 1) + pltpu.roll(x, n - 2, 1)
        return wide(coef[0, s]) * x + wide(coef[1, s]) * near + wide(coef[2, s]) * far

    def mix(x, spots, store_surface):
        hi, lo = split2(x)
        p = jnp.dot(opmat[...], hi, preferred_element_type=F32)
        q = jnp.dot(opmat[0:high], lo, preferred_element_type=F32)
        added = p[0:high] + (p[high : 2 * high] + q)
        mixed = x + added[0:rows]
        flux_now = jnp.tanh(added[rows : rows + 8])
        for i, b in enumerate(spots):
            cols = slice(b * LANES, (b + 1) * LANES)
            part = slice(i * LANES, (i + 1) * LANES)
            s = flux_now[:, part]
            if store_surface:
                kept = s
                if b == 0:
                    kept = jnp.where((sub < fields) & (lane < 2), 0.0, kept)
                    kept = jnp.where((sub >= 4) & (sub < 6) & (lane == sub - 4), 1.0, kept)
                if b == ntile - 1:
                    kept = jnp.where((sub < fields) & (lane >= LANES - 2), 0.0, kept)
                    kept = jnp.where((sub >= 6) & (lane == LANES - 8 + sub), 1.0, kept)
                surf[b] = kept
            for k in range(fields):
                base = k * lev
                out[base : base + lev - 8, cols] = mixed[base : base + lev - 8, part]
                moved = pltpu.roll(s, 7 - k, 0)
                low = sub == 7
                out[base + lev - 8 : base + lev, cols] = mixed[base + lev - 8 : base + lev, part] - jnp.where(
                    low, half * moved, 0.0
                )

    loads[2].wait()
    for i in range(groups):
        s = slice(8 * i, 8 * i + 8)
        out[s, :] = stencil(f[s, LANES : LANES + cells], i)
    pl.semaphore_wait(
        barrier,
        jnp.where(helper, 3, 2) + jnp.where(
            is_atmos,
            jnp.where(spot < HALF, spot + 1 + REACH, 1 + jnp.maximum(spot - (PLANE - 1 - REACH), 0)),
            (comps - 1) * jnp.maximum(spot - (PLANE - 1 - REACH), 0),
        ),
    )

    def pack_copy(way, src, dst, send, recv_at, who):
        return pltpu.make_async_remote_copy(
            src_ref=src,
            dst_ref=dst,
            send_sem=send,
            recv_sem=recv_at,
            device_id=(c, lax.rem(who + tiles, tiles)),
            device_id_type=MESH,
        )

    to_right = pack_copy(0, pack, halo.at[0], halo_send.at[0], halo_recv.at[0], t + 1)
    to_left = pack_copy(1, pack, halo.at[1], halo_send.at[1], halo_recv.at[1], t - 1)
    to_relay = pack_copy(1, pack, relay, relay_send.at[0], relay_recv.at[0], t + PLANE - 1)
    onward = pack_copy(1, relay, halo.at[1], relay_send.at[1], halo_recv.at[1], t - PLANE)

    to_right.start()

    @pl.when(is_ocean)
    def _():
        for d in range(1, REACH + 1):

            @pl.when(spot + d >= PLANE)
            def _():
                for src in range(comps - 1):
                    who = (src, lax.rem(t + d, tiles))
                    pl.semaphore_signal(known.at[4], inc=1, device_id=who, device_id_type=MESH)

    @pl.when(jnp.logical_not(start))
    def _():
        to_left.start()

    @pl.when(start)
    def _():
        to_relay.start()

    @pl.when(helper)
    def _():
        to_relay.wait_recv()
        onward.start()

    for j in range(0, cells, 2 * LANES):
        mix(out[:, j : j + 2 * LANES], (j // LANES, j // LANES + 1), True)
    loads[6].wait()
    loads[7].wait()
    loads[8].wait()
    loads[9].wait()
    loads[10].wait()

    @pl.when(is_atmos)
    def _():
        for n in range(nb):
            picked = surf[ablk_s[n]].astype(BF16)
            part = jnp.dot(picked, w_v[n], preferred_element_type=F32)
            contrib[pl.ds(n, 8, stride=nb), :] = part

    to_right.wait_recv()
    to_left.wait_recv()

    def dense_copy(d):
        return pltpu.make_async_remote_copy(
            src_ref=dense.at[pl.ds((d + REACH) * oblocks, oblocks)],
            dst_ref=recv.at[c * SPREAD + d + REACH],
            send_sem=dense_send.at[d + REACH],
            recv_sem=dense_recv.at[c * SPREAD + d + REACH],
            device_id=(ocean_row, lax.rem(t + d + tiles, tiles)),
            device_id_type=MESH,
        )

    @pl.when(is_atmos)
    def _():
        x = jnp.where(place_in < 2, pltpu.roll(halo[0], LANES - 10, 1), pack[...])
        x = jnp.where(place_in >= 12, pltpu.roll(halo[1], 10, 1), x)
        near = pltpu.roll(x, 1, 1) + pltpu.roll(x, LANES - 1, 1)
        far = pltpu.roll(x, 2, 1) + pltpu.roll(x, LANES - 2, 1)
        z = packed_ops[3] * (packed_ops[0] * x + packed_ops[1] * near + packed_ops[2] * far)
        for shift in (4, 2, 1):
            z = z + pltpu.roll(z, shift, 0)
        z = z + pltpu.roll(z, LANES - GROUP, 1)
        r = jnp.tanh(z).astype(BF16).astype(F32)
        place = toff_v[...] * oblocks + oblk_v[...]
        onehot = (iota((SPREAD * oblocks, nb), 0) == jnp.broadcast_to(place, (SPREAD * oblocks, nb))).astype(F32)
        onehot = onehot.astype(BF16)
        for k in range(fields):
            got = contrib[nb * k : nb * k + nb, :]
            for e, p in enumerate((2, 3, 10, 11)):
                at = 2 * k * GROUP + p
                scale = jnp.broadcast_to(r[:, at : at + 1], (8, LANES))
                scale = jnp.concatenate([scale] * (nb // 8), axis=0)
                got = got + scale * contrib[nb * (4 + e) : nb * (5 + e), :]
            hi, lo = split2(got)
            dense[:, k * LANES : (k + 1) * LANES] = jnp.dot(onehot, hi, preferred_element_type=F32) + jnp.dot(
                onehot, lo, preferred_element_type=F32
            )
        for d in range(1, REACH + 1):

            @pl.when(spot + d >= PLANE)
            def _():
                dense_copy(d).start()

        def inside(d):
            return (spot + d >= 0) & (spot + d < PLANE)

        def send(d, wanted):
            @pl.when(wanted)
            def _():
                dense_copy(d).start()

        def tell(stage, who, wanted):
            @pl.when(wanted)
            def _():
                pl.semaphore_signal(known.at[stage], inc=1, device_id=(c, who), device_id_type=MESH)

        upper = spot >= HALF
        tell(0, right, (spot >= HALF - 1) & (spot < PLANE - 1))
        tell(1, left, (spot == HALF + 1) | (spot == HALF + 2))
        for d in (0, -1, 1):
            send(d, inside(d))
        for d in (-2, 2, -3, 3):
            send(d, inside(d) & jnp.logical_not(upper))

        @pl.when(spot < REACH)
        def _():
            pl.semaphore_wait(known.at[4], REACH - spot)
            for d in range(1, REACH + 1):
                send(-d, spot < d)

        @pl.when(upper)
        def _():
            pl.semaphore_wait(known.at[0], 1)
            tell(2, right, spot < PLANE - 1)
            dense_copy(-2).start()

            @pl.when(spot < HALF + 2)
            def _():
                pl.semaphore_wait(known.at[1], 1)
                tell(3, left, spot == HALF + 1)
                dense_copy(2).start()

            @pl.when(spot > HALF)
            def _():
                pl.semaphore_wait(known.at[2], 1)

            dense_copy(-3).start()

            @pl.when(spot == HALF)
            def _():
                pl.semaphore_wait(known.at[3], 1)
                dense_copy(3).start()

    hl = halo[0]
    hr = halo[1]
    for i in range(groups):
        s = slice(8 * i, 8 * i + 8)
        f[s, 0:LANES] = pltpu.roll(hl, (116 - GROUP * i) % LANES, 1)
        f[s, LANES + cells : 2 * LANES + cells] = pltpu.roll(hr, 126 - GROUP * i, 1)
    lefts, rights = [], []
    for i in range(groups):
        s = slice(8 * i, 8 * i + 8)
        lefts.append(stencil(f[s, 0 : 3 * LANES], i)[:, LANES : 2 * LANES])
        rights.append(stencil(f[s, cells - LANES : cells + 2 * LANES], i)[:, LANES : 2 * LANES])
    edge = jnp.concatenate([jnp.concatenate(lefts, axis=0), jnp.concatenate(rights, axis=0)], axis=1)
    mix(edge, (0, ntile - 1), False)

    to_right.wait_send()

    @pl.when(jnp.logical_not(start))
    def _():
        to_left.wait_send()

    @pl.when(start)
    def _():
        to_relay.wait_send()

    @pl.when(helper)
    def _():
        onward.wait_send()

    @pl.when(is_atmos)
    def _():
        for d in range(-REACH, REACH + 1):
            dense_copy(d).wait_send()

    @pl.when(is_ocean)
    def _():
        total = None
        for slot in sorted(range((comps - 1) * SPREAD), key=lambda slot: slot % SPREAD):
            pltpu.make_async_remote_copy(
                src_ref=dense.at[pl.ds(0, oblocks)],
                dst_ref=recv.at[slot],
                send_sem=dense_send.at[0],
                recv_sem=dense_recv.at[slot],
                device_id=(c, t),
                device_id_type=MESH,
            ).wait_recv()
            total = recv[slot] if total is None else total + recv[slot]
        land = mask_v[...].astype(F32)
        rx[...] = total * jnp.concatenate([land] * fields, axis=1)
        for k in range(fields):
            for o in range(oblocks):
                cols = slice(o * LANES, (o + 1) * LANES)
                out[k * lev : k * lev + 1, cols] += rx[o : o + 1, k * LANES : (k + 1) * LANES]


def solution(mesh):
    comps, tiles = mesh.shape["comp"], mesh.shape["tile"]

    def local(column_state, mixing, vertical, flux_coef, atm_block, ocean_block, tile_offset, remap_weights, ocean_mask):
        fields, lev, cells = column_state.shape[2:]
        nb = remap_weights.shape[2]
        rows = fields * lev
        oblocks = cells // LANES
        dims = (fields, lev, cells, comps, tiles, nb)
        result = pl.pallas_call(
            functools.partial(kernel, dims),
            out_shape=pltpu.VMEM((rows, cells), F32),
            in_specs=[pl.BlockSpec(memory_space=pl.ANY)] * 9,
            out_specs=pl.BlockSpec(memory_space=pltpu.VMEM),
            scratch_shapes=[
                pltpu.VMEM((rows, cells + 2 * LANES), F32),
                pltpu.VMEM(mixing.shape, F32),
                pltpu.VMEM(vertical.shape, F32),
                pltpu.VMEM(flux_coef.shape, F32),
                pltpu.SMEM((nb,), jnp.int32),
                pltpu.VMEM((1, nb), jnp.int32),
                pltpu.VMEM((1, nb), jnp.int32),
                pltpu.VMEM((nb, LANES, LANES), BF16),
                pltpu.VMEM((oblocks, LANES), jnp.int32),
                pltpu.VMEM((3, rows, LANES), F32),
                pltpu.VMEM((2 * (rows + SURF), rows), BF16),
                pltpu.VMEM((8, LANES), F32),
                pltpu.VMEM((2, 8, LANES), F32),
                pltpu.VMEM((oblocks, 8, LANES), F32),
                pltpu.VMEM((8 * nb, LANES), F32),
                pltpu.VMEM((SPREAD * oblocks, fields * LANES), F32),
                pltpu.VMEM(((comps - 1) * SPREAD, oblocks, fields * LANES), F32),
                pltpu.VMEM((8, LANES), F32),
                pltpu.VMEM((4, 8, LANES), F32),
                pltpu.VMEM((oblocks, fields * LANES), F32),
                pltpu.SemaphoreType.DMA((11,)),
                pltpu.SemaphoreType.DMA((2,)),
                pltpu.SemaphoreType.DMA((2,)),
                pltpu.SemaphoreType.DMA((2,)),
                pltpu.SemaphoreType.DMA((1,)),
                pltpu.SemaphoreType.DMA((SPREAD,)),
                pltpu.SemaphoreType.DMA(((comps - 1) * SPREAD,)),
                pltpu.SemaphoreType.REGULAR((5,)),
            ],
            compiler_params=pltpu.CompilerParams(collective_id=0, has_side_effects=True),
            name="step",
        )(
            column_state.reshape(rows, cells),
            mixing,
            vertical,
            flux_coef,
            atm_block.reshape(nb),
            ocean_block.reshape(1, nb),
            tile_offset.reshape(1, nb),
            remap_weights.reshape(remap_weights.shape[2:]),
            ocean_mask.reshape(oblocks, LANES),
        )
        return result.reshape(column_state.shape)

    placed = (
        P("comp", "tile", None, None, None),
        P(),
        P(),
        P(),
        P("comp", "tile", None),
        P("comp", "tile", None),
        P("comp", "tile", None),
        P("comp", "tile", None, None, None),
        P("tile", None),
    )
    return jax.shard_map(
        local,
        mesh=mesh,
        in_specs=placed,
        out_specs=P("comp", "tile", None, None, None),
        check_vma=False,
    )
```

```python
import functools

import jax
import jax.numpy as jnp
from jax import lax
from jax.experimental import pallas as pl
from jax.experimental.pallas import tpu as pltpu
from jax.sharding import PartitionSpec as P

REACH = 3
SPREAD = 2 * REACH + 1
MESH = pl.DeviceIdType.MESH
F32 = jnp.float32
BF16 = jnp.bfloat16
HALF = 4
PLANE = 8
LANES = 128
SURF = 16
GROUP = 16


def iota(shape, dim):
    return lax.broadcasted_iota(jnp.int32, shape, dim)


def column(row, count):
    wide = jnp.broadcast_to(row, (count, row.shape[1]))
    keep = iota(wide.shape, 0) == iota(wide.shape, 1)
    return jnp.sum(jnp.where(keep, wide, 0.0), axis=1, keepdims=True)


def split2(x):
    hi = x.astype(BF16)
    lo = (x - hi.astype(F32)).astype(BF16)
    return hi, lo


def kernel(
    dims,
    state,
    mixing,
    vertical,
    flux,
    ablk,
    oblk,
    toff,
    weights,
    mask,
    out,
    f,
    mix_v,
    ver_v,
    flux_v,
    ablk_s,
    oblk_v,
    toff_v,
    w_v,
    mask_v,
    coef,
    opmat,
    pack,
    halo,
    surf,
    contrib,
    dense,
    recv,
    packed_ops,
    beside,
    seam,
    seam_got,
    seam_pack,
    seam_r,
    relay,
    onehot_v,
    rx,
    load_sem,
    halo_send,
    halo_recv,
    seam_send,
    seam_recv,
    pack_send,
    pack_recv,
    relay_send,
    relay_recv,
    dense_send,
    dense_recv,
    known,
):
    fields, lev, cells, comps, tiles, nb = dims
    rows = fields * lev
    ntile = cells // LANES
    oblocks = cells // LANES
    c = lax.axis_index("comp")
    t = lax.axis_index("tile")
    ocean_row = comps - 1
    is_atmos = c < ocean_row
    is_ocean = c == ocean_row
    group = jnp.where(is_atmos, 0, 1)
    left = lax.rem(t + tiles - 1, tiles)
    right = lax.rem(t + 1, tiles)

    loads = [
        pltpu.make_async_copy(state.at[:, pl.ds(0, LANES)], f.at[:, pl.ds(LANES, LANES)], load_sem.at[0]),
        pltpu.make_async_copy(
            state.at[:, pl.ds(cells - LANES, LANES)], f.at[:, pl.ds(cells, LANES)], load_sem.at[1]
        ),
        pltpu.make_async_copy(
            state.at[:, pl.ds(LANES, cells - 2 * LANES)],
            f.at[:, pl.ds(2 * LANES, cells - 2 * LANES)],
            load_sem.at[2],
        ),
        pltpu.make_async_copy(mixing, mix_v, load_sem.at[3]),
        pltpu.make_async_copy(vertical, ver_v, load_sem.at[4]),
        pltpu.make_async_copy(flux, flux_v, load_sem.at[5]),
        pltpu.make_async_copy(ablk, ablk_s, load_sem.at[6]),
        pltpu.make_async_copy(oblk, oblk_v, load_sem.at[7]),
        pltpu.make_async_copy(toff, toff_v, load_sem.at[8]),
        pltpu.make_async_copy(weights, w_v, load_sem.at[9]),
        pltpu.make_async_copy(mask, mask_v, load_sem.at[10]),
    ]
    barrier = pltpu.get_barrier_semaphore()
    spot = lax.rem(t, PLANE)
    start = t == 0
    end = t == tiles - 1
    ocean_start = (t < REACH + 1) | (t >= tiles - REACH)
    ocean_end = (t < REACH) | (t >= tiles - REACH - 1)
    near_seam = ocean_start | ocean_end
    helper = t == PLANE - 1
    lower = (spot < HALF) | (t < PLANE)

    def greet(row, who):
        pl.semaphore_signal(barrier, inc=1, device_id=(row, lax.rem(who + tiles, tiles)), device_id_type=MESH)

    greet(c, t - 1)

    @pl.when(jnp.logical_not(end))
    def _():
        greet(c, t + 1)

    @pl.when(helper)
    def _():
        greet(c, t - PLANE + 1)
        greet(c, t - PLANE)

    for load in loads:
        load.start()

    @pl.when(is_atmos)
    def _():
        for d in range(1, REACH + 1):

            @pl.when(spot < d)
            def _():
                greet(ocean_row, t - d)

        @pl.when(start)
        def _():
            greet(ocean_row, t - REACH - 1)

    @pl.when(is_ocean)
    def _():
        for d in range(-REACH, REACH + 1):
            there = spot - d
            wanted = (there >= 0) & (there < PLANE)
            if d:
                wanted = wanted & ((there < HALF) | (t < PLANE))
            if d > 0:
                wanted = wanted | (there < 0)

            @pl.when(wanted)
            def _():
                for src in range(comps - 1):
                    greet(src, t - d)

        @pl.when(t == REACH)
        def _():
            for src in range(comps - 1):
                greet(src, t - REACH - 1)

    loads[0].wait()
    loads[1].wait()
    lane = iota((8, LANES), 1)
    sub = iota((8, LANES), 0)
    place_in = lane % GROUP
    groups = rows // 8
    packed = jnp.zeros((8, LANES), F32)
    for i in range(groups):
        here = lane // GROUP == i
        a = f[8 * i : 8 * i + 8, LANES : 2 * LANES]
        b = f[8 * i : 8 * i + 8, cells : cells + LANES]
        packed = jnp.where(here & (place_in < 7), pltpu.roll(a, GROUP * i + 2, 1), packed)
        packed = jnp.where(here & (place_in >= 7), pltpu.roll(b, (GROUP * i + 12) % LANES, 1), packed)
    pack[...] = packed

    loads[3].wait()
    loads[4].wait()
    loads[5].wait()
    def rate_column(mix_g):
        return jnp.concatenate([column(mix_g[k : k + 1, :], lev) for k in range(fields)], axis=0)

    rates = rate_column(mix_v[group])
    keep = 1.0 - 2.0 * rates
    coef[0] = jnp.broadcast_to(keep * keep + 2.0 * rates * rates, (rows, LANES))
    coef[1] = jnp.broadcast_to(2.0 * rates * keep, (rows, LANES))
    coef[2] = jnp.broadcast_to(rates * rates, (rows, LANES))
    spread = (lax.rem(iota((lev, rows), 1), lev) == iota((lev, rows), 0)).astype(F32)
    stacked = jnp.concatenate([ver_v[group]] * fields + [ver_v[0][lev - 8 : lev]], axis=0)
    wide = jnp.dot(stacked, spread, precision=lax.Precision.HIGHEST, preferred_element_type=F32)
    square = jnp.where(iota((rows, rows), 0) // lev == iota((rows, rows), 1) // lev, wide[0:rows], 0.0)
    fa = jnp.concatenate([column(flux_v[0:1, :], fields), jnp.zeros((SURF - fields, 1), F32)], axis=0)
    fb = jnp.concatenate([column(flux_v[1:2, :], fields), jnp.zeros((SURF - fields, 1), F32)], axis=0)
    who_row, who_col = iota((SURF, rows), 0), iota((SURF, rows), 1)
    level = who_col % lev
    top = jnp.where(level == lev - 1, 1.0, 0.0) + wide[rows + 7 : rows + 8]
    under = jnp.where(level == lev - 2, 1.0, 0.0) + wide[rows + 6 : rows + 7]
    linear = jnp.where(who_col // lev == who_row, fa * top + fb * under, 0.0)
    high = rows + SURF
    sq_hi, sq_lo = split2(jnp.concatenate([square, linear], axis=0))
    opmat[0:high] = sq_hi
    opmat[high : 2 * high] = sq_lo
    half = jnp.where(is_atmos, 0.5, 0.0)

    def packed_column(v):
        got = jnp.zeros((8, LANES), F32)
        for i in range(groups):
            got = jnp.where(lane // GROUP == i, jnp.broadcast_to(v[8 * i : 8 * i + 8], (8, LANES)), got)
        return got

    pr = packed_column(rate_column(mix_v[0]))
    pk = 1.0 - 2.0 * pr
    lin = packed_column(column(jnp.sum(linear, axis=0, keepdims=True), rows))
    packed_ops[0] = pk * pk + 2.0 * pr * pr
    packed_ops[1] = 2.0 * pr * pk
    packed_ops[2] = pr * pr
    packed_ops[3] = lin

    def stencil(x, i):
        n = x.shape[1]
        s = slice(8 * i, 8 * i + 8)
        wide = lambda v: jnp.concatenate([v] * (n // LANES), axis=1)
        near = pltpu.roll(x, 1, 1) + pltpu.roll(x, n - 1, 1)
        far = pltpu.roll(x, 2, 1) + pltpu.roll(x, n - 2, 1)
        return wide(coef[0, s]) * x + wide(coef[1, s]) * near + wide(coef[2, s]) * far

    def mix(x, spots, store_surface):
        hi, lo = split2(x)
        p = jnp.dot(opmat[...], hi, preferred_element_type=F32)
        q = jnp.dot(opmat[0:high], lo, preferred_element_type=F32)
        added = p[0:high] + (p[high : 2 * high] + q)
        mixed = x + added[0:rows]
        flux_now = jnp.tanh(added[rows : rows + 8])
        for i, b in enumerate(spots):
            cols = slice(b * LANES, (b + 1) * LANES)
            part = slice(i * LANES, (i + 1) * LANES)
            s = flux_now[:, part]
            if store_surface:
                kept = s
                if b == 0:
                    kept = jnp.where((sub < fields) & (lane < 2), 0.0, kept)
                    kept = jnp.where((sub >= 4) & (sub < 6) & (lane == sub - 4), 1.0, kept)
                if b == ntile - 1:
                    kept = jnp.where((sub < fields) & (lane >= LANES - 2), 0.0, kept)
                    kept = jnp.where((sub >= 6) & (lane == LANES - 8 + sub), 1.0, kept)
                surf[b] = kept
            for k in range(fields):
                base = k * lev
                out[base : base + lev - 8, cols] = mixed[base : base + lev - 8, part]
                moved = pltpu.roll(s, 7 - k, 0)
                low = sub == 7
                out[base + lev - 8 : base + lev, cols] = mixed[base + lev - 8 : base + lev, part] - jnp.where(
                    low, half * moved, 0.0
                )

    pl.semaphore_wait(
        barrier,
        jnp.where(end, 3, 2)
        + jnp.where(
            is_atmos,
            jnp.where(lower, 1 + REACH + jnp.minimum(spot, PLANE - 1 - spot), 1)
            + jnp.maximum(spot - (PLANE - 1 - REACH), 0)
            + jnp.where(end, 1, 0),
            (comps - 1) * (jnp.maximum(spot - (PLANE - 1 - REACH), 0) + jnp.where(t == tiles - REACH - 1, 1, 0)),
        ),
    )

    def pack_copy(way, who):
        return pltpu.make_async_remote_copy(
            src_ref=pack,
            dst_ref=halo.at[way],
            send_sem=halo_send.at[way],
            recv_sem=halo_recv.at[way],
            device_id=(c, who),
            device_id_type=MESH,
        )

    to_right = pack_copy(0, right)
    to_left = pack_copy(1, left)
    to_right.start()

    to_relay = pltpu.make_async_remote_copy(
        src_ref=pack,
        dst_ref=relay,
        send_sem=relay_send.at[0],
        recv_sem=relay_recv.at[0],
        device_id=(c, PLANE - 1),
        device_id_type=MESH,
    )
    onward = pltpu.make_async_remote_copy(
        src_ref=relay,
        dst_ref=halo.at[1],
        send_sem=relay_send.at[1],
        recv_sem=halo_recv.at[1],
        device_id=(c, tiles - 1),
        device_id_type=MESH,
    )

    @pl.when(jnp.logical_not(start))
    def _():
        to_left.start()

    @pl.when(start)
    def _():
        to_relay.start()

    @pl.when(end)
    def _():
        pl.semaphore_signal(known.at[5], inc=1, device_id=(c, PLANE - 1), device_id_type=MESH)

    side = jnp.where(end, 1, 0)

    def seam_pack_copy(d):
        return pltpu.make_async_remote_copy(
            src_ref=pack,
            dst_ref=seam_pack.at[2 * c + side],
            send_sem=pack_send.at[d + REACH + 1],
            recv_sem=pack_recv.at[2 * c + side],
            device_id=(ocean_row, lax.rem(t + d + tiles, tiles)),
            device_id_type=MESH,
        )

    def seam_copy(d):
        return pltpu.make_async_remote_copy(
            src_ref=seam.at[pl.ds((d + REACH) * oblocks, oblocks)],
            dst_ref=seam_got.at[2 * c + side],
            send_sem=seam_send.at[d + REACH],
            recv_sem=seam_recv.at[2 * c + side],
            device_id=(ocean_row, lax.rem(t + d + tiles, tiles)),
            device_id_type=MESH,
        )

    @pl.when(is_atmos & end)
    def _():
        for d in range(1, REACH + 2):
            seam_pack_copy(d).start()

    @pl.when(is_atmos & start)
    def _():
        for d in range(0, REACH + 1):
            seam_pack_copy(d).start()

    @pl.when(is_ocean)
    def _():
        for d in range(1, REACH + 1):

            @pl.when(spot + d >= PLANE)
            def _():
                for src in range(comps - 1):
                    who = (src, lax.rem(t + d, tiles))
                    pl.semaphore_signal(known.at[4], inc=1, device_id=who, device_id_type=MESH)

        @pl.when(t == tiles - REACH - 1)
        def _():
            for src in range(comps - 1):
                pl.semaphore_signal(known.at[4], inc=1, device_id=(src, 0), device_id_type=MESH)

    loads[2].wait()
    for i in range(groups):
        s = slice(8 * i, 8 * i + 8)
        out[s, :] = stencil(f[s, LANES : LANES + cells], i)
    for j in range(0, cells, 2 * LANES):
        mix(out[:, j : j + 2 * LANES], (j // LANES, j // LANES + 1), True)
    loads[6].wait()
    loads[7].wait()
    loads[8].wait()
    loads[9].wait()
    loads[10].wait()

    @pl.when(is_atmos)
    def _():
        for n in range(nb):
            picked = surf[ablk_s[n]].astype(BF16)
            part = jnp.dot(picked, w_v[n], preferred_element_type=F32)
            contrib[pl.ds(n, 8, stride=nb), :] = part
        place = toff_v[...] * oblocks + oblk_v[...]
        onehot = (iota((SPREAD * oblocks, nb), 0) == jnp.broadcast_to(place, (SPREAD * oblocks, nb))).astype(F32)
        onehot_v[...] = onehot.astype(BF16)
        for at_side, first in ((start, fields), (end, fields + 2)):

            @pl.when(at_side)
            def _():
                for e in range(2):
                    rows_of = contrib[nb * (first + e) : nb * (first + e + 1), :].astype(BF16)
                    seam[:, e * LANES : (e + 1) * LANES] = jnp.dot(
                        onehot.astype(BF16), rows_of, preferred_element_type=F32
                    )

        @pl.when(end)
        def _():
            for d in range(1, REACH + 1):
                seam_copy(d).start()

    @pl.when(jnp.logical_not(start))
    def _():
        to_right.wait_recv()
        beside[0] = halo[0]

    @pl.when(start)
    def _():
        beside[0] = jnp.zeros((8, LANES), F32)

    @pl.when(jnp.logical_not(end))
    def _():
        to_left.wait_recv()
        beside[1] = halo[1]

    @pl.when(end)
    def _():
        beside[1] = jnp.zeros((8, LANES), F32)

    def edge_surface(own, before, after):
        x = jnp.where(place_in < 2, pltpu.roll(before, LANES - 10, 1), own)
        x = jnp.where(place_in >= 12, pltpu.roll(after, 10, 1), x)
        near = pltpu.roll(x, 1, 1) + pltpu.roll(x, LANES - 1, 1)
        far = pltpu.roll(x, 2, 1) + pltpu.roll(x, LANES - 2, 1)
        z = packed_ops[3] * (packed_ops[0] * x + packed_ops[1] * near + packed_ops[2] * far)
        for shift in (4, 2, 1):
            z = z + pltpu.roll(z, shift, 0)
        z = z + pltpu.roll(z, LANES - GROUP, 1)
        return jnp.tanh(z).astype(BF16).astype(F32)

    def spread_lane(r, at, height):
        scale = jnp.broadcast_to(r[:, at : at + 1], (8, LANES))
        return jnp.concatenate([scale] * (height // 8), axis=0)

    def dense_copy(d):
        return pltpu.make_async_remote_copy(
            src_ref=dense.at[pl.ds((d + REACH) * oblocks, oblocks)],
            dst_ref=recv.at[c * SPREAD + d + REACH],
            send_sem=dense_send.at[d + REACH],
            recv_sem=dense_recv.at[c * SPREAD + d + REACH],
            device_id=(ocean_row, lax.rem(t + d + tiles, tiles)),
            device_id_type=MESH,
        )

    @pl.when(is_atmos)
    def _():
        r = edge_surface(pack[...], beside[0], beside[1])
        r = jnp.where(start & (place_in < 4), 0.0, jnp.where(end & (place_in > 9), 0.0, r))
        placed = onehot_v[...]
        for k in range(fields):
            got = contrib[nb * k : nb * k + nb, :]
            for e, p in enumerate((2, 3, 10, 11)):
                at = 2 * k * GROUP + p
                got = got + spread_lane(r, at, nb) * contrib[nb * (4 + e) : nb * (5 + e), :]
            hi, lo = split2(got)
            dense[:, k * LANES : (k + 1) * LANES] = jnp.dot(placed, hi, preferred_element_type=F32) + jnp.dot(
                placed, lo, preferred_element_type=F32
            )
        for d in range(1, REACH + 1):

            @pl.when(spot + d >= PLANE)
            def _():
                dense_copy(d).start()

        def inside(d):
            return (spot + d >= 0) & (spot + d < PLANE)

        def send(d, wanted):
            @pl.when(wanted)
            def _():
                dense_copy(d).start()

            @pl.when(wanted & (start | end))
            def _():
                seam_copy(d).start()

                @pl.when((d < 0) | end)
                def _():
                    seam_pack_copy(d).start()

        def tell(stage, who, wanted):
            @pl.when(wanted)
            def _():
                pl.semaphore_signal(known.at[stage], inc=1, device_id=(c, who), device_id_type=MESH)

        upper = jnp.logical_not(lower)
        tell(0, right, (spot >= HALF - 1) & (spot < PLANE - 1) & (t >= PLANE))
        tell(1, left, (spot > HALF) & (spot < HALF + 3) & (t >= PLANE))
        for d in (0, -1, 1):
            send(d, inside(d))
        for d in (-2, 2, -3, 3):
            send(d, inside(d) & jnp.logical_not(upper))

        @pl.when(spot < REACH)
        def _():
            pl.semaphore_wait(known.at[4], jnp.where(start, REACH + 1, REACH - spot))

            @pl.when(start)
            def _():
                seam_pack_copy(-REACH - 1).start()

            for d in range(1, REACH + 1):
                send(-d, spot < d)

        @pl.when(upper)
        def _():
            pl.semaphore_wait(known.at[0], 1)
            tell(2, right, spot < PLANE - 1)
            send(-2, upper)

            @pl.when(spot < HALF + 2)
            def _():
                pl.semaphore_wait(known.at[1], 1)
                tell(3, left, spot == HALF + 1)
                dense_copy(2).start()

            @pl.when(spot > HALF)
            def _():
                pl.semaphore_wait(known.at[2], 1)

            send(-3, upper)

            @pl.when(spot == HALF)
            def _():
                pl.semaphore_wait(known.at[3], 1)
                dense_copy(3).start()

    @pl.when(start)
    def _():
        to_right.wait_recv()

    @pl.when(helper)
    def _():
        to_relay.wait_recv()
        pl.semaphore_wait(known.at[5], 1)
        onward.start()

    @pl.when(end)
    def _():
        to_left.wait_recv()

    hl = halo[0]
    hr = halo[1]
    for i in range(groups):
        s = slice(8 * i, 8 * i + 8)
        f[s, 0:LANES] = pltpu.roll(hl, (116 - GROUP * i) % LANES, 1)
        f[s, LANES + cells : 2 * LANES + cells] = pltpu.roll(hr, 126 - GROUP * i, 1)
    lefts, rights = [], []
    for i in range(groups):
        s = slice(8 * i, 8 * i + 8)
        lefts.append(stencil(f[s, 0 : 3 * LANES], i)[:, LANES : 2 * LANES])
        rights.append(stencil(f[s, cells - LANES : cells + 2 * LANES], i)[:, LANES : 2 * LANES])
    edge = jnp.concatenate([jnp.concatenate(lefts, axis=0), jnp.concatenate(rights, axis=0)], axis=1)
    mix(edge, (0, ntile - 1), False)

    to_right.wait_send()

    @pl.when(jnp.logical_not(start))
    def _():
        to_left.wait_send()

    @pl.when(start)
    def _():
        to_relay.wait_send()

    @pl.when(helper)
    def _():
        onward.wait_send()

    @pl.when(is_atmos & (start | end))
    def _():
        for d in range(-REACH, REACH + 1):
            seam_copy(d).wait_send()
            seam_pack_copy(d).wait_send()

        @pl.when(start)
        def _():
            seam_pack_copy(-REACH - 1).wait_send()

        @pl.when(end)
        def _():
            seam_pack_copy(REACH + 1).wait_send()

    @pl.when(is_atmos)
    def _():
        for d in range(-REACH, REACH + 1):
            dense_copy(d).wait_send()

    @pl.when(is_ocean)
    def _():
        def seam_part(which):
            for src in range(comps - 1):
                pltpu.make_async_remote_copy(
                    src_ref=seam.at[pl.ds(0, oblocks)],
                    dst_ref=seam_got.at[2 * src + which],
                    send_sem=seam_send.at[0],
                    recv_sem=seam_recv.at[2 * src + which],
                    device_id=(c, t),
                    device_id_type=MESH,
                ).wait_recv()
            for k in range(fields):
                cols = slice(k * LANES, (k + 1) * LANES)
                got = rx[:, cols]
                for src in range(comps - 1):
                    r = seam_r[2 * src + which]
                    for e in range(2):
                        at = 2 * k * GROUP + (2, 10)[which] + e
                        got = got + spread_lane(r, at, oblocks) * seam_got[
                            2 * src + which, :, e * LANES : (e + 1) * LANES
                        ]
                rx[:, cols] = got

        rx[...] = jnp.zeros_like(rx)

        @pl.when(near_seam)
        def _():
            for slot in range(2 * (comps - 1)):
                pltpu.make_async_remote_copy(
                    src_ref=pack,
                    dst_ref=seam_pack.at[slot],
                    send_sem=pack_send.at[0],
                    recv_sem=pack_recv.at[slot],
                    device_id=(c, t),
                    device_id_type=MESH,
                ).wait_recv()
            for src in range(comps - 1):
                first, last = seam_pack[2 * src], seam_pack[2 * src + 1]
                seam_r[2 * src] = edge_surface(first, last, last)
                seam_r[2 * src + 1] = edge_surface(last, first, first)

        @pl.when(ocean_start)
        def _():
            seam_part(0)

        total = rx[...]
        for slot in sorted(range((comps - 1) * SPREAD), key=lambda slot: slot % SPREAD):
            pltpu.make_async_remote_copy(
                src_ref=dense.at[pl.ds(0, oblocks)],
                dst_ref=recv.at[slot],
                send_sem=dense_send.at[0],
                recv_sem=dense_recv.at[slot],
                device_id=(c, t),
                device_id_type=MESH,
            ).wait_recv()
            total = total + recv[slot]
        land = mask_v[...].astype(F32)
        rx[...] = total

        @pl.when(ocean_end)
        def _():
            seam_part(1)

        rx[...] = rx[...] * jnp.concatenate([land] * fields, axis=1)
        for k in range(fields):
            for o in range(oblocks):
                cols = slice(o * LANES, (o + 1) * LANES)
                out[k * lev : k * lev + 1, cols] += rx[o : o + 1, k * LANES : (k + 1) * LANES]


def solution(mesh):
    comps, tiles = mesh.shape["comp"], mesh.shape["tile"]

    def local(column_state, mixing, vertical, flux_coef, atm_block, ocean_block, tile_offset, remap_weights, ocean_mask):
        fields, lev, cells = column_state.shape[2:]
        nb = remap_weights.shape[2]
        rows = fields * lev
        oblocks = cells // LANES
        dims = (fields, lev, cells, comps, tiles, nb)
        result = pl.pallas_call(
            functools.partial(kernel, dims),
            out_shape=pltpu.VMEM((rows, cells), F32),
            in_specs=[pl.BlockSpec(memory_space=pl.ANY)] * 9,
            out_specs=pl.BlockSpec(memory_space=pltpu.VMEM),
            scratch_shapes=[
                pltpu.VMEM((rows, cells + 2 * LANES), F32),
                pltpu.VMEM(mixing.shape, F32),
                pltpu.VMEM(vertical.shape, F32),
                pltpu.VMEM(flux_coef.shape, F32),
                pltpu.SMEM((nb,), jnp.int32),
                pltpu.VMEM((1, nb), jnp.int32),
                pltpu.VMEM((1, nb), jnp.int32),
                pltpu.VMEM((nb, LANES, LANES), BF16),
                pltpu.VMEM((oblocks, LANES), jnp.int32),
                pltpu.VMEM((3, rows, LANES), F32),
                pltpu.VMEM((2 * (rows + SURF), rows), BF16),
                pltpu.VMEM((8, LANES), F32),
                pltpu.VMEM((2, 8, LANES), F32),
                pltpu.VMEM((oblocks, 8, LANES), F32),
                pltpu.VMEM((8 * nb, LANES), F32),
                pltpu.VMEM((SPREAD * oblocks, fields * LANES), F32),
                pltpu.VMEM(((comps - 1) * SPREAD, oblocks, fields * LANES), F32),
                pltpu.VMEM((4, 8, LANES), F32),
                pltpu.VMEM((2, 8, LANES), F32),
                pltpu.VMEM((SPREAD * oblocks, 2 * LANES), F32),
                pltpu.VMEM((2 * (comps - 1), oblocks, 2 * LANES), F32),
                pltpu.VMEM((2 * (comps - 1), 8, LANES), F32),
                pltpu.VMEM((2 * (comps - 1), 8, LANES), F32),
                pltpu.VMEM((8, LANES), F32),
                pltpu.VMEM((SPREAD * oblocks, nb), BF16),
                pltpu.VMEM((oblocks, fields * LANES), F32),
                pltpu.SemaphoreType.DMA((11,)),
                pltpu.SemaphoreType.DMA((2,)),
                pltpu.SemaphoreType.DMA((2,)),
                pltpu.SemaphoreType.DMA((SPREAD,)),
                pltpu.SemaphoreType.DMA((2 * (comps - 1),)),
                pltpu.SemaphoreType.DMA((SPREAD + 2,)),
                pltpu.SemaphoreType.DMA((2 * (comps - 1),)),
                pltpu.SemaphoreType.DMA((2,)),
                pltpu.SemaphoreType.DMA((1,)),
                pltpu.SemaphoreType.DMA((SPREAD,)),
                pltpu.SemaphoreType.DMA(((comps - 1) * SPREAD,)),
                pltpu.SemaphoreType.REGULAR((6,)),
            ],
            compiler_params=pltpu.CompilerParams(collective_id=0, has_side_effects=True),
            name="step",
        )(
            column_state.reshape(rows, cells),
            mixing,
            vertical,
            flux_coef,
            atm_block.reshape(nb),
            ocean_block.reshape(1, nb),
            tile_offset.reshape(1, nb),
            remap_weights.reshape(remap_weights.shape[2:]),
            ocean_mask.reshape(oblocks, LANES),
        )
        return result.reshape(column_state.shape)

    placed = (
        P("comp", "tile", None, None, None),
        P(),
        P(),
        P(),
        P("comp", "tile", None),
        P("comp", "tile", None),
        P("comp", "tile", None),
        P("comp", "tile", None, None, None),
        P("tile", None),
    )
    return jax.shard_map(
        local,
        mesh=mesh,
        in_specs=placed,
        out_specs=P("comp", "tile", None, None, None),
        check_vma=False,
    )
```

```python
import functools

import jax
import jax.numpy as jnp
from jax import lax
from jax.experimental import pallas as pl
from jax.experimental.pallas import tpu as pltpu
from jax.sharding import PartitionSpec as P

REACH = 3
SPREAD = 2 * REACH + 1
MESH = pl.DeviceIdType.MESH
F32 = jnp.float32
BF16 = jnp.bfloat16
HALF = 4
PLANE = 8
LANES = 128
SURF = 16
GROUP = 16


def iota(shape, dim):
    return lax.broadcasted_iota(jnp.int32, shape, dim)


def column(row, count):
    wide = jnp.broadcast_to(row, (count, row.shape[1]))
    keep = iota(wide.shape, 0) == iota(wide.shape, 1)
    return jnp.sum(jnp.where(keep, wide, 0.0), axis=1, keepdims=True)


def split2(x):
    hi = x.astype(BF16)
    lo = (x - hi.astype(F32)).astype(BF16)
    return hi, lo


def kernel(
    dims,
    state,
    mixing,
    vertical,
    flux,
    ablk,
    oblk,
    toff,
    weights,
    mask,
    out,
    f,
    mix_v,
    ver_v,
    flux_v,
    ablk_s,
    oblk_v,
    toff_v,
    w_v,
    mask_v,
    coef,
    opmat,
    pack,
    halo,
    surf,
    contrib,
    dense,
    recv,
    packed_ops,
    beside,
    seam,
    seam_got,
    seam_pack,
    seam_r,
    relay,
    borders,
    rx,
    load_sem,
    halo_send,
    halo_recv,
    seam_send,
    seam_recv,
    pack_send,
    pack_recv,
    relay_send,
    relay_recv,
    dense_send,
    dense_recv,
    known,
):
    fields, lev, cells, comps, tiles, nb = dims
    rows = fields * lev
    ntile = cells // LANES
    oblocks = cells // LANES
    c = lax.axis_index("comp")
    t = lax.axis_index("tile")
    ocean_row = comps - 1
    is_atmos = c < ocean_row
    is_ocean = c == ocean_row
    group = jnp.where(is_atmos, 0, 1)
    left = lax.rem(t + tiles - 1, tiles)
    right = lax.rem(t + 1, tiles)

    loads = [
        pltpu.make_async_copy(state.at[:, pl.ds(0, LANES)], f.at[:, pl.ds(LANES, LANES)], load_sem.at[0]),
        pltpu.make_async_copy(
            state.at[:, pl.ds(cells - LANES, LANES)], f.at[:, pl.ds(cells, LANES)], load_sem.at[1]
        ),
        pltpu.make_async_copy(
            state.at[:, pl.ds(LANES, cells - 2 * LANES)],
            f.at[:, pl.ds(2 * LANES, cells - 2 * LANES)],
            load_sem.at[2],
        ),
        pltpu.make_async_copy(mixing, mix_v, load_sem.at[3]),
        pltpu.make_async_copy(vertical, ver_v, load_sem.at[4]),
        pltpu.make_async_copy(flux, flux_v, load_sem.at[5]),
        pltpu.make_async_copy(ablk, ablk_s, load_sem.at[6]),
        pltpu.make_async_copy(oblk, oblk_v, load_sem.at[7]),
        pltpu.make_async_copy(toff, toff_v, load_sem.at[8]),
        pltpu.make_async_copy(weights, w_v, load_sem.at[9]),
        pltpu.make_async_copy(mask, mask_v, load_sem.at[10]),
    ]
    barrier = pltpu.get_barrier_semaphore()
    spot = lax.rem(t, PLANE)
    start = t == 0
    end = t == tiles - 1
    ocean_start = (t < REACH + 1) | (t >= tiles - REACH)
    ocean_end = (t < REACH) | (t >= tiles - REACH - 1)
    near_seam = ocean_start | ocean_end
    helper = t == PLANE - 1
    lower = (spot < HALF) | (t < PLANE)

    def greet(row, who):
        pl.semaphore_signal(barrier, inc=1, device_id=(row, lax.rem(who + tiles, tiles)), device_id_type=MESH)

    greet(c, t - 1)

    @pl.when(jnp.logical_not(end))
    def _():
        greet(c, t + 1)

    @pl.when(helper)
    def _():
        greet(c, t - PLANE + 1)
        greet(c, t - PLANE)

    for load in loads:
        load.start()

    @pl.when(is_atmos)
    def _():
        for d in range(1, REACH + 1):

            @pl.when(spot < d)
            def _():
                greet(ocean_row, t - d)

        @pl.when(start)
        def _():
            greet(ocean_row, t - REACH - 1)

    @pl.when(is_ocean)
    def _():
        for d in range(-REACH, REACH + 1):
            there = spot - d
            wanted = (there >= 0) & (there < PLANE)
            if d:
                wanted = wanted & ((there < HALF) | (t < PLANE))
            if d > 0:
                wanted = wanted | (there < 0)

            @pl.when(wanted)
            def _():
                for src in range(comps - 1):
                    greet(src, t - d)

        @pl.when(t == REACH)
        def _():
            for src in range(comps - 1):
                greet(src, t - REACH - 1)

    loads[0].wait()
    loads[1].wait()
    lane = iota((8, LANES), 1)
    sub = iota((8, LANES), 0)
    place_in = lane % GROUP
    groups = rows // 8
    packed = jnp.zeros((8, LANES), F32)
    for i in range(groups):
        here = lane // GROUP == i
        a = f[8 * i : 8 * i + 8, LANES : 2 * LANES]
        b = f[8 * i : 8 * i + 8, cells : cells + LANES]
        packed = jnp.where(here & (place_in < 7), pltpu.roll(a, GROUP * i + 2, 1), packed)
        packed = jnp.where(here & (place_in >= 7), pltpu.roll(b, (GROUP * i + 12) % LANES, 1), packed)
    pack[...] = packed

    pl.semaphore_wait(
        barrier,
        jnp.where(end, 3, 2)
        + jnp.where(
            is_atmos,
            jnp.where(lower, 1 + REACH + jnp.minimum(spot, PLANE - 1 - spot), 1)
            + jnp.maximum(spot - (PLANE - 1 - REACH), 0)
            + jnp.where(end, 1, 0),
            (comps - 1) * (jnp.maximum(spot - (PLANE - 1 - REACH), 0) + jnp.where(t == tiles - REACH - 1, 1, 0)),
        ),
    )

    def pack_copy(way, who):
        return pltpu.make_async_remote_copy(
            src_ref=pack,
            dst_ref=halo.at[way],
            send_sem=halo_send.at[way],
            recv_sem=halo_recv.at[way],
            device_id=(c, who),
            device_id_type=MESH,
        )

    to_right = pack_copy(0, right)
    to_left = pack_copy(1, left)
    to_right.start()

    to_relay = pltpu.make_async_remote_copy(
        src_ref=pack,
        dst_ref=relay,
        send_sem=relay_send.at[0],
        recv_sem=relay_recv.at[0],
        device_id=(c, PLANE - 1),
        device_id_type=MESH,
    )
    onward = pltpu.make_async_remote_copy(
        src_ref=relay,
        dst_ref=halo.at[1],
        send_sem=relay_send.at[1],
        recv_sem=halo_recv.at[1],
        device_id=(c, tiles - 1),
        device_id_type=MESH,
    )

    @pl.when(jnp.logical_not(start))
    def _():
        to_left.start()

    @pl.when(start)
    def _():
        to_relay.start()

    @pl.when(end)
    def _():
        pl.semaphore_signal(known.at[5], inc=1, device_id=(c, PLANE - 1), device_id_type=MESH)

    side = jnp.where(end, 1, 0)

    def seam_pack_copy(d):
        return pltpu.make_async_remote_copy(
            src_ref=pack,
            dst_ref=seam_pack.at[2 * c + side],
            send_sem=pack_send.at[d + REACH + 1],
            recv_sem=pack_recv.at[2 * c + side],
            device_id=(ocean_row, lax.rem(t + d + tiles, tiles)),
            device_id_type=MESH,
        )

    def seam_copy(d):
        return pltpu.make_async_remote_copy(
            src_ref=seam.at[pl.ds((d + REACH) * oblocks, oblocks)],
            dst_ref=seam_got.at[2 * c + side],
            send_sem=seam_send.at[d + REACH],
            recv_sem=seam_recv.at[2 * c + side],
            device_id=(ocean_row, lax.rem(t + d + tiles, tiles)),
            device_id_type=MESH,
        )

    @pl.when(is_atmos & end)
    def _():
        for d in range(1, REACH + 2):
            seam_pack_copy(d).start()

    @pl.when(is_atmos & start)
    def _():
        for d in range(0, REACH + 1):
            seam_pack_copy(d).start()

    @pl.when(is_ocean)
    def _():
        for d in range(1, REACH + 1):

            @pl.when(spot + d >= PLANE)
            def _():
                for src in range(comps - 1):
                    who = (src, lax.rem(t + d, tiles))
                    pl.semaphore_signal(known.at[4], inc=1, device_id=who, device_id_type=MESH)

        @pl.when(t == tiles - REACH - 1)
        def _():
            for src in range(comps - 1):
                pl.semaphore_signal(known.at[4], inc=1, device_id=(src, 0), device_id_type=MESH)

    loads[3].wait()
    loads[4].wait()
    loads[5].wait()
    def rate_column(mix_g):
        return jnp.concatenate([column(mix_g[k : k + 1, :], lev) for k in range(fields)], axis=0)

    rates = rate_column(mix_v[group])
    keep = 1.0 - 2.0 * rates
    coef[0] = jnp.broadcast_to(keep * keep + 2.0 * rates * rates, (rows, LANES))
    coef[1] = jnp.broadcast_to(2.0 * rates * keep, (rows, LANES))
    coef[2] = jnp.broadcast_to(rates * rates, (rows, LANES))
    spread = (lax.rem(iota((lev, rows), 1), lev) == iota((lev, rows), 0)).astype(F32)
    stacked = jnp.concatenate([ver_v[group]] * fields + [ver_v[0][lev - 8 : lev]], axis=0)
    wide = jnp.dot(stacked, spread, precision=lax.Precision.HIGHEST, preferred_element_type=F32)
    square = jnp.where(iota((rows, rows), 0) // lev == iota((rows, rows), 1) // lev, wide[0:rows], 0.0)
    fa = jnp.concatenate([column(flux_v[0:1, :], fields), jnp.zeros((SURF - fields, 1), F32)], axis=0)
    fb = jnp.concatenate([column(flux_v[1:2, :], fields), jnp.zeros((SURF - fields, 1), F32)], axis=0)
    who_row, who_col = iota((SURF, rows), 0), iota((SURF, rows), 1)
    level = who_col % lev
    top = jnp.where(level == lev - 1, 1.0, 0.0) + wide[rows + 7 : rows + 8]
    under = jnp.where(level == lev - 2, 1.0, 0.0) + wide[rows + 6 : rows + 7]
    linear = jnp.where(who_col // lev == who_row, fa * top + fb * under, 0.0)
    high = rows + SURF
    sq_hi, sq_lo = split2(jnp.concatenate([square, linear], axis=0))
    opmat[0:high] = sq_hi
    opmat[high : 2 * high] = sq_lo
    half = jnp.where(is_atmos, 0.5, 0.0)

    def packed_column(v):
        got = jnp.zeros((8, LANES), F32)
        for i in range(groups):
            got = jnp.where(lane // GROUP == i, jnp.broadcast_to(v[8 * i : 8 * i + 8], (8, LANES)), got)
        return got

    pr = packed_column(rate_column(mix_v[0]))
    pk = 1.0 - 2.0 * pr
    lin = packed_column(column(jnp.sum(linear, axis=0, keepdims=True), rows))
    packed_ops[0] = pk * pk + 2.0 * pr * pr
    packed_ops[1] = 2.0 * pr * pk
    packed_ops[2] = pr * pr
    packed_ops[3] = lin

    def stencil(x, i):
        n = x.shape[1]
        s = slice(8 * i, 8 * i + 8)
        wide = lambda v: jnp.concatenate([v] * (n // LANES), axis=1)
        near = pltpu.roll(x, 1, 1) + pltpu.roll(x, n - 1, 1)
        far = pltpu.roll(x, 2, 1) + pltpu.roll(x, n - 2, 1)
        return wide(coef[0, s]) * x + wide(coef[1, s]) * near + wide(coef[2, s]) * far

    def mix(x, spots, store_surface):
        hi, lo = split2(x)
        p = jnp.dot(opmat[...], hi, preferred_element_type=F32)
        q = jnp.dot(opmat[0:high], lo, preferred_element_type=F32)
        added = p[0:high] + (p[high : 2 * high] + q)
        mixed = x + added[0:rows]
        flux_now = jnp.tanh(added[rows : rows + 8])
        for i, b in enumerate(spots):
            cols = slice(b * LANES, (b + 1) * LANES)
            part = slice(i * LANES, (i + 1) * LANES)
            s = flux_now[:, part]
            if store_surface:
                kept = s
                if b == 0:
                    kept = jnp.where((sub < fields) & (lane < 2), 0.0, kept)
                    kept = jnp.where((sub >= 4) & (sub < 6) & (lane == sub - 4), 1.0, kept)
                if b == ntile - 1:
                    kept = jnp.where((sub < fields) & (lane >= LANES - 2), 0.0, kept)
                    kept = jnp.where((sub >= 6) & (lane == LANES - 8 + sub), 1.0, kept)
                surf[b] = kept
            for k in range(fields):
                base = k * lev
                out[base : base + lev - 8, cols] = mixed[base : base + lev - 8, part]
                moved = pltpu.roll(s, 7 - k, 0)
                low = sub == 7
                out[base + lev - 8 : base + lev, cols] = mixed[base + lev - 8 : base + lev, part] - jnp.where(
                    low, half * moved, 0.0
                )

    loads[2].wait()
    for i in range(groups):
        s = slice(8 * i, 8 * i + 8)
        out[s, :] = stencil(f[s, LANES : LANES + cells], i)
    for j in range(0, cells, 2 * LANES):
        mix(out[:, j : j + 2 * LANES], (j // LANES, j // LANES + 1), True)
    loads[6].wait()
    loads[7].wait()
    loads[8].wait()
    loads[9].wait()
    loads[10].wait()

    @pl.when(is_atmos)
    def _():
        for n in range(nb):
            picked = surf[ablk_s[n]].astype(BF16)
            part = jnp.dot(picked, w_v[n], preferred_element_type=F32)
            contrib[pl.ds(n, 8, stride=nb), :] = part
        place = toff_v[...] * oblocks + oblk_v[...]
        onehot = (iota((SPREAD * oblocks, nb), 0) == jnp.broadcast_to(place, (SPREAD * oblocks, nb))).astype(F32)
        placed = onehot.astype(BF16)
        hi, lo = split2(contrib[...])
        for k in range(8):
            part_k = slice(nb * k, nb * k + nb)
            got = jnp.dot(placed, hi[part_k], preferred_element_type=F32)
            if k < fields:
                got = got + jnp.dot(placed, lo[part_k], preferred_element_type=F32)
                dense[:, k * LANES : (k + 1) * LANES] = got
            else:
                borders[:, (k - fields) * LANES : (k - fields + 1) * LANES] = got

        @pl.when(start)
        def _():
            seam[...] = borders[:, 0 : 2 * LANES]

        @pl.when(end)
        def _():
            seam[...] = borders[:, 2 * LANES : 4 * LANES]

        @pl.when(end)
        def _():
            for d in range(1, REACH + 1):
                seam_copy(d).start()

    @pl.when(jnp.logical_not(start))
    def _():
        to_right.wait_recv()
        beside[0] = halo[0]

    @pl.when(start)
    def _():
        beside[0] = jnp.zeros((8, LANES), F32)

    @pl.when(jnp.logical_not(end))
    def _():
        to_left.wait_recv()
        beside[1] = halo[1]

    @pl.when(end)
    def _():
        beside[1] = jnp.zeros((8, LANES), F32)

    def edge_surface(own, before, after):
        x = jnp.where(place_in < 2, pltpu.roll(before, LANES - 10, 1), own)
        x = jnp.where(place_in >= 12, pltpu.roll(after, 10, 1), x)
        near = pltpu.roll(x, 1, 1) + pltpu.roll(x, LANES - 1, 1)
        far = pltpu.roll(x, 2, 1) + pltpu.roll(x, LANES - 2, 1)
        z = packed_ops[3] * (packed_ops[0] * x + packed_ops[1] * near + packed_ops[2] * far)
        for shift in (4, 2, 1):
            z = z + pltpu.roll(z, shift, 0)
        z = z + pltpu.roll(z, LANES - GROUP, 1)
        return jnp.tanh(z).astype(BF16).astype(F32)

    def spread_lane(r, at, height):
        scale = jnp.broadcast_to(r[:, at : at + 1], (8, LANES))
        return jnp.concatenate([scale] * (height // 8), axis=0)

    def dense_copy(d):
        return pltpu.make_async_remote_copy(
            src_ref=dense.at[pl.ds((d + REACH) * oblocks, oblocks)],
            dst_ref=recv.at[c * SPREAD + d + REACH],
            send_sem=dense_send.at[d + REACH],
            recv_sem=dense_recv.at[c * SPREAD + d + REACH],
            device_id=(ocean_row, lax.rem(t + d + tiles, tiles)),
            device_id_type=MESH,
        )

    @pl.when(is_atmos)
    def _():
        r = edge_surface(pack[...], beside[0], beside[1])
        r = jnp.where(start & (place_in < 4), 0.0, jnp.where(end & (place_in > 9), 0.0, r))
        scales = [[spread_lane(r, 2 * k * GROUP + p, oblocks) for p in (2, 3, 10, 11)] for k in range(fields)]

        def complete(d):
            part_d = slice((d + REACH) * oblocks, (d + REACH + 1) * oblocks)
            weights_d = [borders[part_d, e * LANES : (e + 1) * LANES] for e in range(4)]
            for k in range(fields):
                got = dense[part_d, k * LANES : (k + 1) * LANES]
                for e in range(4):
                    got = got + scales[k][e] * weights_d[e]
                dense[part_d, k * LANES : (k + 1) * LANES] = got

        for d in range(1, REACH + 1):
            complete(d)
        for d in range(1, REACH + 1):

            @pl.when(spot + d >= PLANE)
            def _():
                dense_copy(d).start()

        for d in range(-REACH, 1):
            complete(d)

        def inside(d):
            return (spot + d >= 0) & (spot + d < PLANE)

        def send(d, wanted):
            @pl.when(wanted)
            def _():
                dense_copy(d).start()

            @pl.when(wanted & (start | end))
            def _():
                seam_copy(d).start()

                @pl.when((d < 0) | end)
                def _():
                    seam_pack_copy(d).start()

        def tell(stage, who, wanted):
            @pl.when(wanted)
            def _():
                pl.semaphore_signal(known.at[stage], inc=1, device_id=(c, who), device_id_type=MESH)

        upper = jnp.logical_not(lower)
        tell(0, right, (spot >= HALF - 1) & (spot < PLANE - 1) & (t >= PLANE))
        tell(1, left, (spot > HALF) & (spot < HALF + 3) & (t >= PLANE))
        for d in (0, -1, 1):
            send(d, inside(d))
        for d in (-2, 2, -3, 3):
            send(d, inside(d) & jnp.logical_not(upper))

        @pl.when((spot < REACH) & jnp.logical_not(start & (c == 0)))
        def _():
            pl.semaphore_wait(known.at[4], jnp.where(start, REACH + 1, REACH - spot))

            @pl.when(start)
            def _():
                seam_pack_copy(-REACH - 1).start()

            for d in range(1, REACH + 1):
                send(-d, spot < d)

        @pl.when(upper)
        def _():
            pl.semaphore_wait(known.at[0], 1)
            tell(2, right, spot < PLANE - 1)
            send(-2, upper)

            @pl.when(spot < HALF + 2)
            def _():
                pl.semaphore_wait(known.at[1], 1)
                tell(3, left, spot == HALF + 1)
                dense_copy(2).start()

            @pl.when(spot > HALF)
            def _():
                pl.semaphore_wait(known.at[2], 1)

            send(-3, upper)

            @pl.when(spot == HALF)
            def _():
                pl.semaphore_wait(known.at[3], 1)
                dense_copy(3).start()

    @pl.when(start)
    def _():
        to_right.wait_recv()

    @pl.when(helper)
    def _():
        to_relay.wait_recv()
        pl.semaphore_wait(known.at[5], 1)
        onward.start()

    @pl.when(end)
    def _():
        to_left.wait_recv()

    hl = halo[0]
    hr = halo[1]
    for i in range(groups):
        s = slice(8 * i, 8 * i + 8)
        f[s, 0:LANES] = pltpu.roll(hl, (116 - GROUP * i) % LANES, 1)
        f[s, LANES + cells : 2 * LANES + cells] = pltpu.roll(hr, 126 - GROUP * i, 1)
    lefts, rights = [], []
    for i in range(groups):
        s = slice(8 * i, 8 * i + 8)
        lefts.append(stencil(f[s, 0 : 3 * LANES], i)[:, LANES : 2 * LANES])
        rights.append(stencil(f[s, cells - LANES : cells + 2 * LANES], i)[:, LANES : 2 * LANES])
    edge = jnp.concatenate([jnp.concatenate(lefts, axis=0), jnp.concatenate(rights, axis=0)], axis=1)
    mix(edge, (0, ntile - 1), False)

    @pl.when(start & (c == 0))
    def _():
        pl.semaphore_wait(known.at[4], REACH + 1)
        seam_pack_copy(-REACH - 1).start()
        for d in range(-1, -REACH - 1, -1):
            dense_copy(d).start()
            seam_copy(d).start()
            seam_pack_copy(d).start()

    to_right.wait_send()

    @pl.when(jnp.logical_not(start))
    def _():
        to_left.wait_send()

    @pl.when(start)
    def _():
        to_relay.wait_send()

    @pl.when(helper)
    def _():
        onward.wait_send()

    @pl.when(is_atmos & (start | end))
    def _():
        for d in range(-REACH, REACH + 1):
            seam_copy(d).wait_send()
            seam_pack_copy(d).wait_send()

        @pl.when(start)
        def _():
            seam_pack_copy(-REACH - 1).wait_send()

        @pl.when(end)
        def _():
            seam_pack_copy(REACH + 1).wait_send()

    @pl.when(is_atmos)
    def _():
        for d in range(-REACH, REACH + 1):
            dense_copy(d).wait_send()

    @pl.when(is_ocean)
    def _():
        def seam_part(which):
            for src in range(comps - 1):
                pltpu.make_async_remote_copy(
                    src_ref=seam.at[pl.ds(0, oblocks)],
                    dst_ref=seam_got.at[2 * src + which],
                    send_sem=seam_send.at[0],
                    recv_sem=seam_recv.at[2 * src + which],
                    device_id=(c, t),
                    device_id_type=MESH,
                ).wait_recv()
            for k in range(fields):
                cols = slice(k * LANES, (k + 1) * LANES)
                got = rx[:, cols]
                for src in range(comps - 1):
                    r = seam_r[2 * src + which]
                    for e in range(2):
                        at = 2 * k * GROUP + (2, 10)[which] + e
                        got = got + spread_lane(r, at, oblocks) * seam_got[
                            2 * src + which, :, e * LANES : (e + 1) * LANES
                        ]
                rx[:, cols] = got

        rx[...] = jnp.zeros_like(rx)

        @pl.when(near_seam)
        def _():
            for slot in range(2 * (comps - 1)):
                pltpu.make_async_remote_copy(
                    src_ref=pack,
                    dst_ref=seam_pack.at[slot],
                    send_sem=pack_send.at[0],
                    recv_sem=pack_recv.at[slot],
                    device_id=(c, t),
                    device_id_type=MESH,
                ).wait_recv()
            for src in range(comps - 1):
                first, last = seam_pack[2 * src], seam_pack[2 * src + 1]
                seam_r[2 * src] = edge_surface(first, last, last)
                seam_r[2 * src + 1] = edge_surface(last, first, first)

        @pl.when(ocean_start)
        def _():
            seam_part(0)

        total = rx[...]
        for slot in sorted(range((comps - 1) * SPREAD), key=lambda slot: slot % SPREAD):
            pltpu.make_async_remote_copy(
                src_ref=dense.at[pl.ds(0, oblocks)],
                dst_ref=recv.at[slot],
                send_sem=dense_send.at[0],
                recv_sem=dense_recv.at[slot],
                device_id=(c, t),
                device_id_type=MESH,
            ).wait_recv()
            total = total + recv[slot]
        land = mask_v[...].astype(F32)
        rx[...] = total

        @pl.when(ocean_end)
        def _():
            seam_part(1)

        rx[...] = rx[...] * jnp.concatenate([land] * fields, axis=1)
        for k in range(fields):
            for o in range(oblocks):
                cols = slice(o * LANES, (o + 1) * LANES)
                out[k * lev : k * lev + 1, cols] += rx[o : o + 1, k * LANES : (k + 1) * LANES]


def solution(mesh):
    comps, tiles = mesh.shape["comp"], mesh.shape["tile"]

    def local(column_state, mixing, vertical, flux_coef, atm_block, ocean_block, tile_offset, remap_weights, ocean_mask):
        fields, lev, cells = column_state.shape[2:]
        nb = remap_weights.shape[2]
        rows = fields * lev
        oblocks = cells // LANES
        dims = (fields, lev, cells, comps, tiles, nb)
        result = pl.pallas_call(
            functools.partial(kernel, dims),
            out_shape=pltpu.VMEM((rows, cells), F32),
            in_specs=[pl.BlockSpec(memory_space=pl.ANY)] * 9,
            out_specs=pl.BlockSpec(memory_space=pltpu.VMEM),
            scratch_shapes=[
                pltpu.VMEM((rows, cells + 2 * LANES), F32),
                pltpu.VMEM(mixing.shape, F32),
                pltpu.VMEM(vertical.shape, F32),
                pltpu.VMEM(flux_coef.shape, F32),
                pltpu.SMEM((nb,), jnp.int32),
                pltpu.VMEM((1, nb), jnp.int32),
                pltpu.VMEM((1, nb), jnp.int32),
                pltpu.VMEM((nb, LANES, LANES), BF16),
                pltpu.VMEM((oblocks, LANES), jnp.int32),
                pltpu.VMEM((3, rows, LANES), F32),
                pltpu.VMEM((2 * (rows + SURF), rows), BF16),
                pltpu.VMEM((8, LANES), F32),
                pltpu.VMEM((2, 8, LANES), F32),
                pltpu.VMEM((oblocks, 8, LANES), F32),
                pltpu.VMEM((8 * nb, LANES), F32),
                pltpu.VMEM((SPREAD * oblocks, fields * LANES), F32),
                pltpu.VMEM(((comps - 1) * SPREAD, oblocks, fields * LANES), F32),
                pltpu.VMEM((4, 8, LANES), F32),
                pltpu.VMEM((2, 8, LANES), F32),
                pltpu.VMEM((SPREAD * oblocks, 2 * LANES), F32),
                pltpu.VMEM((2 * (comps - 1), oblocks, 2 * LANES), F32),
                pltpu.VMEM((2 * (comps - 1), 8, LANES), F32),
                pltpu.VMEM((2 * (comps - 1), 8, LANES), F32),
                pltpu.VMEM((8, LANES), F32),
                pltpu.VMEM((SPREAD * oblocks, 4 * LANES), F32),
                pltpu.VMEM((oblocks, fields * LANES), F32),
                pltpu.SemaphoreType.DMA((11,)),
                pltpu.SemaphoreType.DMA((2,)),
                pltpu.SemaphoreType.DMA((2,)),
                pltpu.SemaphoreType.DMA((SPREAD,)),
                pltpu.SemaphoreType.DMA((2 * (comps - 1),)),
                pltpu.SemaphoreType.DMA((SPREAD + 2,)),
                pltpu.SemaphoreType.DMA((2 * (comps - 1),)),
                pltpu.SemaphoreType.DMA((2,)),
                pltpu.SemaphoreType.DMA((1,)),
                pltpu.SemaphoreType.DMA((SPREAD,)),
                pltpu.SemaphoreType.DMA(((comps - 1) * SPREAD,)),
                pltpu.SemaphoreType.REGULAR((6,)),
            ],
            compiler_params=pltpu.CompilerParams(collective_id=0, has_side_effects=True),
            name="step",
        )(
            column_state.reshape(rows, cells),
            mixing,
            vertical,
            flux_coef,
            atm_block.reshape(nb),
            ocean_block.reshape(1, nb),
            tile_offset.reshape(1, nb),
            remap_weights.reshape(remap_weights.shape[2:]),
            ocean_mask.reshape(oblocks, LANES),
        )
        return result.reshape(column_state.shape)

    placed = (
        P("comp", "tile", None, None, None),
        P(),
        P(),
        P(),
        P("comp", "tile", None),
        P("comp", "tile", None),
        P("comp", "tile", None),
        P("comp", "tile", None, None, None),
        P("tile", None),
    )
    return jax.shard_map(
        local,
        mesh=mesh,
        in_specs=placed,
        out_specs=P("comp", "tile", None, None, None),
        check_vma=False,
    )
```

```python
import functools

import jax
import jax.numpy as jnp
from jax import lax
from jax.experimental import pallas as pl
from jax.experimental.pallas import tpu as pltpu
from jax.sharding import PartitionSpec as P

REACH = 3
SPREAD = 2 * REACH + 1
MESH = pl.DeviceIdType.MESH
F32 = jnp.float32
BF16 = jnp.bfloat16
HALF = 4
PLANE = 8
LANES = 128
SURF = 16
GROUP = 16


def iota(shape, dim):
    return lax.broadcasted_iota(jnp.int32, shape, dim)


def column(row, count):
    wide = jnp.broadcast_to(row, (count, row.shape[1]))
    keep = iota(wide.shape, 0) == iota(wide.shape, 1)
    return jnp.sum(jnp.where(keep, wide, 0.0), axis=1, keepdims=True)


def split2(x):
    hi = x.astype(BF16)
    lo = (x - hi.astype(F32)).astype(BF16)
    return hi, lo


def kernel(
    dims,
    state,
    mixing,
    vertical,
    flux,
    ablk,
    oblk,
    toff,
    weights,
    mask,
    out,
    f,
    mix_v,
    ver_v,
    flux_v,
    ablk_s,
    oblk_v,
    toff_v,
    w_v,
    mask_v,
    coef,
    opmat,
    pack,
    halo,
    surf,
    contrib,
    dense,
    recv,
    packed_ops,
    beside,
    seam,
    seam_got,
    seam_pack,
    seam_r,
    relay,
    borders,
    base,
    rx,
    load_sem,
    halo_send,
    halo_recv,
    seam_send,
    seam_recv,
    pack_send,
    pack_recv,
    relay_send,
    relay_recv,
    dense_send,
    dense_recv,
    known,
):
    fields, lev, cells, comps, tiles, nb = dims
    rows = fields * lev
    ntile = cells // LANES
    oblocks = cells // LANES
    c = lax.axis_index("comp")
    t = lax.axis_index("tile")
    ocean_row = comps - 1
    is_atmos = c < ocean_row
    is_ocean = c == ocean_row
    group = jnp.where(is_atmos, 0, 1)
    left = lax.rem(t + tiles - 1, tiles)
    right = lax.rem(t + 1, tiles)

    loads = [
        pltpu.make_async_copy(state.at[:, pl.ds(0, LANES)], f.at[:, pl.ds(LANES, LANES)], load_sem.at[0]),
        pltpu.make_async_copy(
            state.at[:, pl.ds(cells - LANES, LANES)], f.at[:, pl.ds(cells, LANES)], load_sem.at[1]
        ),
        pltpu.make_async_copy(
            state.at[:, pl.ds(LANES, cells - 2 * LANES)],
            f.at[:, pl.ds(2 * LANES, cells - 2 * LANES)],
            load_sem.at[2],
        ),
        pltpu.make_async_copy(mixing, mix_v, load_sem.at[3]),
        pltpu.make_async_copy(vertical, ver_v, load_sem.at[4]),
        pltpu.make_async_copy(flux, flux_v, load_sem.at[5]),
        pltpu.make_async_copy(ablk, ablk_s, load_sem.at[6]),
        pltpu.make_async_copy(oblk, oblk_v, load_sem.at[7]),
        pltpu.make_async_copy(toff, toff_v, load_sem.at[8]),
        pltpu.make_async_copy(weights, w_v, load_sem.at[9]),
        pltpu.make_async_copy(mask, mask_v, load_sem.at[10]),
    ]
    barrier = pltpu.get_barrier_semaphore()
    spot = lax.rem(t, PLANE)
    start = t == 0
    end = t == tiles - 1
    ocean_start = (t < REACH + 1) | (t >= tiles - REACH)
    ocean_end = (t < REACH) | (t >= tiles - REACH - 1)
    near_seam = ocean_start | ocean_end
    helper = t == PLANE - 1
    lower = (spot < HALF) | (t < PLANE)

    def greet(row, who):
        pl.semaphore_signal(barrier, inc=1, device_id=(row, lax.rem(who + tiles, tiles)), device_id_type=MESH)

    greet(c, t - 1)

    @pl.when(jnp.logical_not(end))
    def _():
        greet(c, t + 1)

    @pl.when(helper)
    def _():
        greet(c, t - PLANE + 1)
        greet(c, t - PLANE)

    for load in loads:
        load.start()

    @pl.when(is_atmos)
    def _():
        for d in range(1, REACH + 1):

            @pl.when(spot < d)
            def _():
                greet(ocean_row, t - d)

        @pl.when(start)
        def _():
            greet(ocean_row, t - REACH - 1)

    @pl.when(is_ocean)
    def _():
        for d in range(-REACH, REACH + 1):
            there = spot - d
            wanted = (there >= 0) & (there < PLANE)
            if d:
                wanted = wanted & ((there < HALF) | (t < PLANE))
            if d > 0:
                wanted = wanted | (there < 0)

            @pl.when(wanted)
            def _():
                for src in range(comps - 1):
                    greet(src, t - d)

        @pl.when(t == REACH)
        def _():
            for src in range(comps - 1):
                greet(src, t - REACH - 1)

    loads[0].wait()
    loads[1].wait()
    lane = iota((8, LANES), 1)
    sub = iota((8, LANES), 0)
    place_in = lane % GROUP
    groups = rows // 8
    packed = jnp.zeros((8, LANES), F32)
    for i in range(groups):
        here = lane // GROUP == i
        a = f[8 * i : 8 * i + 8, LANES : 2 * LANES]
        b = f[8 * i : 8 * i + 8, cells : cells + LANES]
        packed = jnp.where(here & (place_in < 7), pltpu.roll(a, GROUP * i + 2, 1), packed)
        packed = jnp.where(here & (place_in >= 7), pltpu.roll(b, (GROUP * i + 12) % LANES, 1), packed)
    pack[...] = packed

    pl.semaphore_wait(
        barrier,
        jnp.where(end, 3, 2)
        + jnp.where(
            is_atmos,
            jnp.where(lower, 1 + REACH + jnp.minimum(spot, PLANE - 1 - spot), 1)
            + jnp.maximum(spot - (PLANE - 1 - REACH), 0)
            + jnp.where(end, 1, 0),
            (comps - 1) * (jnp.maximum(spot - (PLANE - 1 - REACH), 0) + jnp.where(t == tiles - REACH - 1, 1, 0)),
        ),
    )

    def pack_copy(way, who):
        return pltpu.make_async_remote_copy(
            src_ref=pack,
            dst_ref=halo.at[way],
            send_sem=halo_send.at[way],
            recv_sem=halo_recv.at[way],
            device_id=(c, who),
            device_id_type=MESH,
        )

    to_right = pack_copy(0, right)
    to_left = pack_copy(1, left)
    to_right.start()

    to_relay = pltpu.make_async_remote_copy(
        src_ref=pack,
        dst_ref=relay,
        send_sem=relay_send.at[0],
        recv_sem=relay_recv.at[0],
        device_id=(c, PLANE - 1),
        device_id_type=MESH,
    )
    onward = pltpu.make_async_remote_copy(
        src_ref=relay,
        dst_ref=halo.at[1],
        send_sem=relay_send.at[1],
        recv_sem=halo_recv.at[1],
        device_id=(c, tiles - 1),
        device_id_type=MESH,
    )

    @pl.when(jnp.logical_not(start))
    def _():
        to_left.start()

    @pl.when(start)
    def _():
        to_relay.start()

    @pl.when(end)
    def _():
        pl.semaphore_signal(known.at[5], inc=1, device_id=(c, PLANE - 1), device_id_type=MESH)

    side = jnp.where(end, 1, 0)

    def seam_pack_copy(d):
        return pltpu.make_async_remote_copy(
            src_ref=pack,
            dst_ref=seam_pack.at[2 * c + side],
            send_sem=pack_send.at[d + REACH + 1],
            recv_sem=pack_recv.at[2 * c + side],
            device_id=(ocean_row, lax.rem(t + d + tiles, tiles)),
            device_id_type=MESH,
        )

    def seam_copy(d):
        return pltpu.make_async_remote_copy(
            src_ref=seam.at[pl.ds((d + REACH) * oblocks, oblocks)],
            dst_ref=seam_got.at[2 * c + side],
            send_sem=seam_send.at[d + REACH],
            recv_sem=seam_recv.at[2 * c + side],
            device_id=(ocean_row, lax.rem(t + d + tiles, tiles)),
            device_id_type=MESH,
        )

    @pl.when(is_atmos & end)
    def _():
        for d in range(1, REACH + 2):
            seam_pack_copy(d).start()

    @pl.when(is_atmos & start)
    def _():
        for d in range(0, REACH + 1):
            seam_pack_copy(d).start()

    @pl.when(is_ocean)
    def _():
        for d in range(1, REACH + 1):

            @pl.when(spot + d >= PLANE)
            def _():
                for src in range(comps - 1):
                    who = (src, lax.rem(t + d, tiles))
                    pl.semaphore_signal(known.at[4], inc=1, device_id=who, device_id_type=MESH)

        @pl.when(t == tiles - REACH - 1)
        def _():
            for src in range(comps - 1):
                pl.semaphore_signal(known.at[4], inc=1, device_id=(src, 0), device_id_type=MESH)

    loads[3].wait()
    loads[4].wait()
    loads[5].wait()
    def rate_column(mix_g):
        return jnp.concatenate([column(mix_g[k : k + 1, :], lev) for k in range(fields)], axis=0)

    rates = rate_column(mix_v[group])
    keep = 1.0 - 2.0 * rates
    coef[0] = jnp.broadcast_to(keep * keep + 2.0 * rates * rates, (rows, LANES))
    coef[1] = jnp.broadcast_to(2.0 * rates * keep, (rows, LANES))
    coef[2] = jnp.broadcast_to(rates * rates, (rows, LANES))
    spread = (lax.rem(iota((lev, rows), 1), lev) == iota((lev, rows), 0)).astype(F32)
    stacked = jnp.concatenate([ver_v[group]] * fields + [ver_v[0][lev - 8 : lev]], axis=0)
    wide = jnp.dot(stacked, spread, precision=lax.Precision.HIGHEST, preferred_element_type=F32)
    square = jnp.where(iota((rows, rows), 0) // lev == iota((rows, rows), 1) // lev, wide[0:rows], 0.0)
    fa = jnp.concatenate([column(flux_v[0:1, :], fields), jnp.zeros((SURF - fields, 1), F32)], axis=0)
    fb = jnp.concatenate([column(flux_v[1:2, :], fields), jnp.zeros((SURF - fields, 1), F32)], axis=0)
    who_row, who_col = iota((SURF, rows), 0), iota((SURF, rows), 1)
    level = who_col % lev
    top = jnp.where(level == lev - 1, 1.0, 0.0) + wide[rows + 7 : rows + 8]
    under = jnp.where(level == lev - 2, 1.0, 0.0) + wide[rows + 6 : rows + 7]
    linear = jnp.where(who_col // lev == who_row, fa * top + fb * under, 0.0)
    high = rows + SURF
    sq_hi, sq_lo = split2(jnp.concatenate([square, linear], axis=0))
    opmat[0:high] = sq_hi
    opmat[high : 2 * high] = sq_lo
    half = jnp.where(is_atmos, 0.5, 0.0)

    def packed_column(v):
        got = jnp.zeros((8, LANES), F32)
        for i in range(groups):
            got = jnp.where(lane // GROUP == i, jnp.broadcast_to(v[8 * i : 8 * i + 8], (8, LANES)), got)
        return got

    pr = packed_column(rate_column(mix_v[0]))
    pk = 1.0 - 2.0 * pr
    lin = packed_column(column(jnp.sum(linear, axis=0, keepdims=True), rows))
    packed_ops[0] = pk * pk + 2.0 * pr * pr
    packed_ops[1] = 2.0 * pr * pk
    packed_ops[2] = pr * pr
    packed_ops[3] = lin

    def stencil(x, i):
        n = x.shape[1]
        s = slice(8 * i, 8 * i + 8)
        wide = lambda v: jnp.concatenate([v] * (n // LANES), axis=1)
        near = pltpu.roll(x, 1, 1) + pltpu.roll(x, n - 1, 1)
        far = pltpu.roll(x, 2, 1) + pltpu.roll(x, n - 2, 1)
        return wide(coef[0, s]) * x + wide(coef[1, s]) * near + wide(coef[2, s]) * far

    def mix(x, spots, store_surface):
        hi, lo = split2(x)
        p = jnp.dot(opmat[...], hi, preferred_element_type=F32)
        q = jnp.dot(opmat[0:high], lo, preferred_element_type=F32)
        added = p[0:high] + (p[high : 2 * high] + q)
        mixed = x + added[0:rows]
        flux_now = jnp.tanh(added[rows : rows + 8])
        for i, b in enumerate(spots):
            cols = slice(b * LANES, (b + 1) * LANES)
            part = slice(i * LANES, (i + 1) * LANES)
            s = flux_now[:, part]
            if store_surface:
                kept = s
                if b == 0:
                    kept = jnp.where((sub < fields) & (lane < 2), 0.0, kept)
                    kept = jnp.where((sub >= 4) & (sub < 6) & (lane == sub - 4), 1.0, kept)
                if b == ntile - 1:
                    kept = jnp.where((sub < fields) & (lane >= LANES - 2), 0.0, kept)
                    kept = jnp.where((sub >= 6) & (lane == LANES - 8 + sub), 1.0, kept)
                surf[b] = kept
            for k in range(fields):
                base = k * lev
                out[base : base + lev - 8, cols] = mixed[base : base + lev - 8, part]
                moved = pltpu.roll(s, 7 - k, 0)
                low = sub == 7
                out[base + lev - 8 : base + lev, cols] = mixed[base + lev - 8 : base + lev, part] - jnp.where(
                    low, half * moved, 0.0
                )

    loads[2].wait()
    for i in range(groups):
        s = slice(8 * i, 8 * i + 8)
        out[s, :] = stencil(f[s, LANES : LANES + cells], i)
    for j in range(0, cells, 2 * LANES):
        mix(out[:, j : j + 2 * LANES], (j // LANES, j // LANES + 1), True)
    loads[6].wait()
    loads[7].wait()
    loads[8].wait()
    loads[9].wait()
    loads[10].wait()

    @pl.when(is_atmos)
    def _():
        for n in range(nb):
            picked = surf[ablk_s[n]].astype(BF16)
            part = jnp.dot(picked, w_v[n], preferred_element_type=F32)
            contrib[pl.ds(n, 8, stride=nb), :] = part
        place = toff_v[...] * oblocks + oblk_v[...]
        onehot = (iota((SPREAD * oblocks, nb), 0) == jnp.broadcast_to(place, (SPREAD * oblocks, nb))).astype(F32)
        placed = onehot.astype(BF16)
        hi, lo = split2(contrib[...])
        for k in range(8):
            part_k = slice(nb * k, nb * k + nb)
            got = jnp.dot(placed, hi[part_k], preferred_element_type=F32)
            if k < fields:
                got = got + jnp.dot(placed, lo[part_k], preferred_element_type=F32)
                dense[:, k * LANES : (k + 1) * LANES] = got
            else:
                borders[:, (k - fields) * LANES : (k - fields + 1) * LANES] = got

        @pl.when(start)
        def _():
            seam[...] = borders[:, 0 : 2 * LANES]

        @pl.when(end)
        def _():
            seam[...] = borders[:, 2 * LANES : 4 * LANES]

        @pl.when(end)
        def _():
            for d in range(1, REACH + 1):
                seam_copy(d).start()

    @pl.when(jnp.logical_not(start))
    def _():
        to_right.wait_recv()
        beside[0] = halo[0]

    @pl.when(start)
    def _():
        beside[0] = jnp.zeros((8, LANES), F32)

    @pl.when(jnp.logical_not(end))
    def _():
        to_left.wait_recv()
        beside[1] = halo[1]

    @pl.when(end)
    def _():
        beside[1] = jnp.zeros((8, LANES), F32)

    def edge_surface(own, before, after):
        x = jnp.where(place_in < 2, pltpu.roll(before, LANES - 10, 1), own)
        x = jnp.where(place_in >= 12, pltpu.roll(after, 10, 1), x)
        near = pltpu.roll(x, 1, 1) + pltpu.roll(x, LANES - 1, 1)
        far = pltpu.roll(x, 2, 1) + pltpu.roll(x, LANES - 2, 1)
        z = packed_ops[3] * (packed_ops[0] * x + packed_ops[1] * near + packed_ops[2] * far)
        for shift in (4, 2, 1):
            z = z + pltpu.roll(z, shift, 0)
        z = z + pltpu.roll(z, LANES - GROUP, 1)
        return jnp.tanh(z).astype(BF16).astype(F32)

    def spread_lane(r, at, height):
        scale = jnp.broadcast_to(r[:, at : at + 1], (8, LANES))
        return jnp.concatenate([scale] * (height // 8), axis=0)

    def dense_copy(d):
        return pltpu.make_async_remote_copy(
            src_ref=dense.at[pl.ds((d + REACH) * oblocks, oblocks)],
            dst_ref=recv.at[c * SPREAD + d + REACH],
            send_sem=dense_send.at[d + REACH],
            recv_sem=dense_recv.at[c * SPREAD + d + REACH],
            device_id=(ocean_row, lax.rem(t + d + tiles, tiles)),
            device_id_type=MESH,
        )

    @pl.when(is_atmos)
    def _():
        r = edge_surface(pack[...], beside[0], beside[1])
        r = jnp.where(start & (place_in < 4), 0.0, jnp.where(end & (place_in > 9), 0.0, r))
        scales = [[spread_lane(r, 2 * k * GROUP + p, oblocks) for p in (2, 3, 10, 11)] for k in range(fields)]

        def complete(d):
            part_d = slice((d + REACH) * oblocks, (d + REACH + 1) * oblocks)
            weights_d = [borders[part_d, e * LANES : (e + 1) * LANES] for e in range(4)]
            for k in range(fields):
                got = dense[part_d, k * LANES : (k + 1) * LANES]
                for e in range(4):
                    got = got + scales[k][e] * weights_d[e]
                dense[part_d, k * LANES : (k + 1) * LANES] = got

        for d in range(1, REACH + 1):
            complete(d)

            @pl.when(spot + d >= PLANE)
            def _():
                dense_copy(d).start()

        for d in range(-REACH, 1):
            complete(d)

        def inside(d):
            return (spot + d >= 0) & (spot + d < PLANE)

        def send(d, wanted):
            @pl.when(wanted)
            def _():
                dense_copy(d).start()

            @pl.when(wanted & (start | end))
            def _():
                seam_copy(d).start()

                @pl.when((d < 0) | end)
                def _():
                    seam_pack_copy(d).start()

        def tell(stage, who, wanted):
            @pl.when(wanted)
            def _():
                pl.semaphore_signal(known.at[stage], inc=1, device_id=(c, who), device_id_type=MESH)

        upper = jnp.logical_not(lower)
        tell(0, right, (spot >= HALF - 1) & (spot < PLANE - 1) & (t >= PLANE))
        tell(1, left, (spot > HALF) & (spot < HALF + 3) & (t >= PLANE))
        for d in (0, -1, 1):
            send(d, inside(d))
        for d in (-2, 2, -3, 3):
            send(d, inside(d) & jnp.logical_not(upper))

        @pl.when((spot < REACH) & jnp.logical_not(start & (c == 0)))
        def _():
            pl.semaphore_wait(known.at[4], jnp.where(start, REACH + 1, REACH - spot))

            @pl.when(start)
            def _():
                seam_pack_copy(-REACH - 1).start()

            for d in range(1, REACH + 1):
                send(-d, spot < d)

        @pl.when(upper)
        def _():
            pl.semaphore_wait(known.at[0], 1)
            tell(2, right, spot < PLANE - 1)
            send(-2, upper)

            @pl.when(spot < HALF + 2)
            def _():
                pl.semaphore_wait(known.at[1], 1)
                tell(3, left, spot == HALF + 1)
                dense_copy(2).start()

            @pl.when(spot > HALF)
            def _():
                pl.semaphore_wait(known.at[2], 1)

            send(-3, upper)

            @pl.when(spot == HALF)
            def _():
                pl.semaphore_wait(known.at[3], 1)
                dense_copy(3).start()

    @pl.when(start)
    def _():
        to_right.wait_recv()

    @pl.when(helper)
    def _():
        to_relay.wait_recv()
        pl.semaphore_wait(known.at[5], 1)
        onward.start()

    @pl.when(end)
    def _():
        to_left.wait_recv()

    hl = halo[0]
    hr = halo[1]
    for i in range(groups):
        s = slice(8 * i, 8 * i + 8)
        f[s, 0:LANES] = pltpu.roll(hl, (116 - GROUP * i) % LANES, 1)
        f[s, LANES + cells : 2 * LANES + cells] = pltpu.roll(hr, 126 - GROUP * i, 1)
    lefts, rights = [], []
    for i in range(groups):
        s = slice(8 * i, 8 * i + 8)
        lefts.append(stencil(f[s, 0 : 3 * LANES], i)[:, LANES : 2 * LANES])
        rights.append(stencil(f[s, cells - LANES : cells + 2 * LANES], i)[:, LANES : 2 * LANES])
    edge = jnp.concatenate([jnp.concatenate(lefts, axis=0), jnp.concatenate(rights, axis=0)], axis=1)
    mix(edge, (0, ntile - 1), False)

    @pl.when(start & (c == 0))
    def _():
        pl.semaphore_wait(known.at[4], REACH + 1)
        seam_pack_copy(-REACH - 1).start()
        for d in range(-1, -REACH - 1, -1):
            dense_copy(d).start()
            seam_copy(d).start()
            seam_pack_copy(d).start()

    to_right.wait_send()

    @pl.when(jnp.logical_not(start))
    def _():
        to_left.wait_send()

    @pl.when(start)
    def _():
        to_relay.wait_send()

    @pl.when(helper)
    def _():
        onward.wait_send()

    @pl.when(is_atmos & (start | end))
    def _():
        for d in range(-REACH, REACH + 1):
            seam_copy(d).wait_send()
            seam_pack_copy(d).wait_send()

        @pl.when(start)
        def _():
            seam_pack_copy(-REACH - 1).wait_send()

        @pl.when(end)
        def _():
            seam_pack_copy(REACH + 1).wait_send()

    @pl.when(is_atmos)
    def _():
        for d in range(-REACH, REACH + 1):
            dense_copy(d).wait_send()

    @pl.when(is_ocean)
    def _():
        def seam_part(which):
            for src in range(comps - 1):
                pltpu.make_async_remote_copy(
                    src_ref=seam.at[pl.ds(0, oblocks)],
                    dst_ref=seam_got.at[2 * src + which],
                    send_sem=seam_send.at[0],
                    recv_sem=seam_recv.at[2 * src + which],
                    device_id=(c, t),
                    device_id_type=MESH,
                ).wait_recv()
            for k in range(fields):
                cols = slice(k * LANES, (k + 1) * LANES)
                got = rx[:, cols]
                for src in range(comps - 1):
                    r = seam_r[2 * src + which]
                    for e in range(2):
                        at = 2 * k * GROUP + (2, 10)[which] + e
                        got = got + spread_lane(r, at, oblocks) * seam_got[
                            2 * src + which, :, e * LANES : (e + 1) * LANES
                        ]
                rx[:, cols] = got

        rx[...] = jnp.zeros_like(rx)

        @pl.when(near_seam)
        def _():
            for slot in range(2 * (comps - 1)):
                pltpu.make_async_remote_copy(
                    src_ref=pack,
                    dst_ref=seam_pack.at[slot],
                    send_sem=pack_send.at[0],
                    recv_sem=pack_recv.at[slot],
                    device_id=(c, t),
                    device_id_type=MESH,
                ).wait_recv()
            for src in range(comps - 1):
                first, last = seam_pack[2 * src], seam_pack[2 * src + 1]
                seam_r[2 * src] = edge_surface(first, last, last)
                seam_r[2 * src + 1] = edge_surface(last, first, first)

        @pl.when(ocean_start)
        def _():
            seam_part(0)

        @pl.when(ocean_end)
        def _():
            seam_part(1)

        for k in range(fields):
            for o in range(oblocks):
                base[o : o + 1, k * LANES : (k + 1) * LANES] = out[
                    k * lev : k * lev + 1, o * LANES : (o + 1) * LANES
                ]
        total = rx[...]
        for slot in sorted(range((comps - 1) * SPREAD), key=lambda slot: slot % SPREAD):
            pltpu.make_async_remote_copy(
                src_ref=dense.at[pl.ds(0, oblocks)],
                dst_ref=recv.at[slot],
                send_sem=dense_send.at[0],
                recv_sem=dense_recv.at[slot],
                device_id=(c, t),
                device_id_type=MESH,
            ).wait_recv()
            total = total + recv[slot]
        land = mask_v[...].astype(F32)
        rx[...] = base[...] + total * jnp.concatenate([land] * fields, axis=1)
        for k in range(fields):
            for o in range(oblocks):
                cols = slice(o * LANES, (o + 1) * LANES)
                out[k * lev : k * lev + 1, cols] = rx[o : o + 1, k * LANES : (k + 1) * LANES]


def solution(mesh):
    comps, tiles = mesh.shape["comp"], mesh.shape["tile"]

    def local(column_state, mixing, vertical, flux_coef, atm_block, ocean_block, tile_offset, remap_weights, ocean_mask):
        fields, lev, cells = column_state.shape[2:]
        nb = remap_weights.shape[2]
        rows = fields * lev
        oblocks = cells // LANES
        dims = (fields, lev, cells, comps, tiles, nb)
        result = pl.pallas_call(
            functools.partial(kernel, dims),
            out_shape=pltpu.VMEM((rows, cells), F32),
            in_specs=[pl.BlockSpec(memory_space=pl.ANY)] * 9,
            out_specs=pl.BlockSpec(memory_space=pltpu.VMEM),
            scratch_shapes=[
                pltpu.VMEM((rows, cells + 2 * LANES), F32),
                pltpu.VMEM(mixing.shape, F32),
                pltpu.VMEM(vertical.shape, F32),
                pltpu.VMEM(flux_coef.shape, F32),
                pltpu.SMEM((nb,), jnp.int32),
                pltpu.VMEM((1, nb), jnp.int32),
                pltpu.VMEM((1, nb), jnp.int32),
                pltpu.VMEM((nb, LANES, LANES), BF16),
                pltpu.VMEM((oblocks, LANES), jnp.int32),
                pltpu.VMEM((3, rows, LANES), F32),
                pltpu.VMEM((2 * (rows + SURF), rows), BF16),
                pltpu.VMEM((8, LANES), F32),
                pltpu.VMEM((2, 8, LANES), F32),
                pltpu.VMEM((oblocks, 8, LANES), F32),
                pltpu.VMEM((8 * nb, LANES), F32),
                pltpu.VMEM((SPREAD * oblocks, fields * LANES), F32),
                pltpu.VMEM(((comps - 1) * SPREAD, oblocks, fields * LANES), F32),
                pltpu.VMEM((4, 8, LANES), F32),
                pltpu.VMEM((2, 8, LANES), F32),
                pltpu.VMEM((SPREAD * oblocks, 2 * LANES), F32),
                pltpu.VMEM((2 * (comps - 1), oblocks, 2 * LANES), F32),
                pltpu.VMEM((2 * (comps - 1), 8, LANES), F32),
                pltpu.VMEM((2 * (comps - 1), 8, LANES), F32),
                pltpu.VMEM((8, LANES), F32),
                pltpu.VMEM((SPREAD * oblocks, 4 * LANES), F32),
                pltpu.VMEM((oblocks, fields * LANES), F32),
                pltpu.VMEM((oblocks, fields * LANES), F32),
                pltpu.SemaphoreType.DMA((11,)),
                pltpu.SemaphoreType.DMA((2,)),
                pltpu.SemaphoreType.DMA((2,)),
                pltpu.SemaphoreType.DMA((SPREAD,)),
                pltpu.SemaphoreType.DMA((2 * (comps - 1),)),
                pltpu.SemaphoreType.DMA((SPREAD + 2,)),
                pltpu.SemaphoreType.DMA((2 * (comps - 1),)),
                pltpu.SemaphoreType.DMA((2,)),
                pltpu.SemaphoreType.DMA((1,)),
                pltpu.SemaphoreType.DMA((SPREAD,)),
                pltpu.SemaphoreType.DMA(((comps - 1) * SPREAD,)),
                pltpu.SemaphoreType.REGULAR((6,)),
            ],
            compiler_params=pltpu.CompilerParams(collective_id=0, has_side_effects=True),
            name="step",
        )(
            column_state.reshape(rows, cells),
            mixing,
            vertical,
            flux_coef,
            atm_block.reshape(nb),
            ocean_block.reshape(1, nb),
            tile_offset.reshape(1, nb),
            remap_weights.reshape(remap_weights.shape[2:]),
            ocean_mask.reshape(oblocks, LANES),
        )
        return result.reshape(column_state.shape)

    placed = (
        P("comp", "tile", None, None, None),
        P(),
        P(),
        P(),
        P("comp", "tile", None),
        P("comp", "tile", None),
        P("comp", "tile", None),
        P("comp", "tile", None, None, None),
        P("tile", None),
    )
    return jax.shard_map(
        local,
        mesh=mesh,
        in_specs=placed,
        out_specs=P("comp", "tile", None, None, None),
        check_vma=False,
    )
```
